512 devices in a mesh: ev: 64 (over z, x_lo, core), uni: 8 (over x_hi, y).
Axes of the slice: x: 4 (x_hi: 2, x_lo: 2; x = x_hi * 2 + x_lo), y: 4, z: 16, core: 2. Of those that a mesh axis runs over, the one named last changes fastest.
Arguments:
- responses: bfloat16 [64, 1048576], P(None, 'ev'), may hold values from -0.25 to 0.25
- event_bins: int32 [1048576], P('ev'), may hold values from 0 to 4095, as said below
- nominal_weight: bfloat16 [1048576], P('ev'), may hold values from 0.5 to 2
- throws: int32 [64, 1024], P(None, 'uni'), may hold values from -2 to 2
Outputs:
- spectra: float32 [4096, 1024], P('ev', 'uni')
- covariance: float32 [4096, 4096], P('uni', 'ev')
The draws below stay inside these ranges and needn't reach their ends.
Inputs may be any that keep to these rules, and one draw needn't show every extreme that they name: `event_bins`: within the 16384 events of each device, in order, the bins never fall.
All inputs are finite; a program needn't handle non-finite values.
Results may differ from the reference program's by a relative error of at most 0.00042.
Values sent between devices are 32-bit elements; how exact they have to be, the bound alone decides.
A program may use at most 64 MiB of HBM per device.

```python
import math
import jax
import jax.numpy as jnp
from jax import lax

KNOBS = 64
UNIVERSES = 1024
BINS = 4096
EV_DEV = 16384
EVENTS = 1048576
N_UNI = 8


def draw_event_bins(key, part):
    drawn_bins = jax.random.randint(key, (EVENTS,), 0, BINS, dtype=jnp.int32)
    return jnp.sort(drawn_bins.reshape(-1, EV_DEV), axis=1).reshape(EVENTS)


def place_ends(entries, rng, low, top_value):
    shape = entries.shape
    index_at = [jax.random.randint(jax.random.fold_in(rng, axis), (), 0, shape[axis]) for axis in range(len(shape))]
    entries = entries.at[tuple(index_at)].set(low)
    longest = shape.index(max(shape))
    index_at[longest] = (index_at[longest] + 1) % shape[longest]
    return entries.at[tuple(index_at)].set(top_value)


def levels(stream_key, dims, pieces, low, top_value):
    factor_of = 1.0
    for position, parts in pieces:
        steps = jax.random.uniform(jax.random.fold_in(jax.random.fold_in(stream_key, 6), position), (parts,), jnp.float32, low / len(pieces), top_value / len(pieces))
        factor_of = factor_of * jnp.repeat(jnp.exp(steps), dims[position] // parts).reshape((-1,) + (1,) * (len(dims) - 1 - position))
    return factor_of


def noise(own_key, shape, scale, bound, pieces=(), held_as=jnp.bfloat16):
    drawn = scale * jax.random.normal(own_key, shape, jnp.float32)
    if pieces:
        drawn = drawn * levels(own_key, shape, pieces, -0.22, 0.18)
    return jnp.clip(drawn, -bound, bound).astype(held_as)


def setup_inputs(seed: int = 0) -> dict:
    splits = jax.random.split(jax.random.key(seed), 5)
    responses = noise(splits[0], (KNOBS, EVENTS), 0.09, 0.25, ((1, 64),))
    event_bins = draw_event_bins(jax.random.fold_in(splits[4], 71), 0)
    nominal_weight = jnp.clip(jnp.exp(math.log(2.0) - 1.3862944 * jax.random.uniform(splits[2], (EVENTS,), jnp.float32) ** levels(splits[2], (EVENTS,), ((0, 64),), -0.2, 0.2)), 0.5, 2.0).astype(jnp.bfloat16)
    throws = place_ends(jax.random.randint(splits[3], (KNOBS, UNIVERSES), -2, 3), jax.random.fold_in(splits[3], 1), -2, 2).astype(jnp.int32)
    return {"responses": responses, "event_bins": event_bins, "nominal_weight": nominal_weight, "throws": throws}


def reference(responses, event_bins, nominal_weight, throws):
    per_bin = EVENTS // BINS
    group_width = UNIVERSES // N_UNI
    event_major = responses.T
    nominal_float = nominal_weight.astype(jnp.float32)
    central = jax.ops.segment_sum(nominal_float, event_bins, BINS)
    throw_groups = throws.reshape(KNOBS, N_UNI, group_width).transpose(1, 0, 2)

    def one_group(throw_block):
        log_weight = jnp.dot(event_major, throw_block.astype(jnp.bfloat16), preferred_element_type=jnp.float32)
        weights = (nominal_float[:, None] * jnp.exp(log_weight)).astype(jnp.bfloat16)
        return jax.ops.segment_sum(weights.astype(jnp.float32), event_bins, BINS)

    grouped = lax.map(one_group, throw_groups)
    histogram = grouped.transpose(1, 0, 2).reshape(BINS, UNIVERSES)
    deviation = histogram - central[:, None]
    gram = jnp.dot(deviation, deviation.T, precision=lax.Precision.HIGHEST, preferred_element_type=jnp.float32)
    covariance = gram / (UNIVERSES * per_bin)
    spectra = histogram / per_bin
    return spectra, covariance
```

```python
import functools

import jax
import jax.numpy as jnp
from jax import lax
from jax.experimental import pallas as pl
from jax.experimental.pallas import tpu as pltpu
from jax.sharding import PartitionSpec as P

LANES = 128
QUARTER = 32
BLOCK_ROWS = 72
CHUNK = 512
MESH = pl.DeviceIdType.MESH
F32 = jnp.float32


def hist_kernel(edges, resp, bins, nominal, throws_t, out, acc, weights):
    tiles = acc.shape[0] - 1
    chunks = resp.shape[1] // CHUNK
    zero_tile = jnp.zeros(acc.shape[1:], F32)

    def clear(t, carry):
        acc[t] = zero_tile
        return carry

    lax.fori_loop(0, tiles + 1, clear, 0)
    knob_throws = throws_t[...]
    bin_iota = lax.broadcasted_iota(jnp.int32, (2 * LANES, CHUNK), 0)

    def add_window(tile, bin_row):
        onehot = jnp.where(bin_iota == bin_row - tile * LANES, 1.0, 0.0).astype(jnp.bfloat16)
        part = lax.dot_general(
            weights[...], onehot, (((1,), (1,)), ((), ())), preferred_element_type=F32
        )
        acc[tile] += part[:, :LANES]
        acc[tile + 1] += part[:, LANES:]

    def step(i, carry):
        at = pl.ds(pl.multiple_of(i * CHUNK, CHUNK), CHUNK)
        nominal_row = nominal[:, at]
        log_weight = jnp.dot(knob_throws, resp[:, at], preferred_element_type=F32)
        weights[: 4 * QUARTER] = (nominal_row * jnp.exp(log_weight)).astype(jnp.bfloat16)
        weights[4 * QUARTER :] = jnp.broadcast_to(nominal_row, (16, CHUNK)).astype(jnp.bfloat16)
        bin_row = bins[:, at]
        first = edges[i, 0] // LANES
        last = edges[i, 1] // LANES
        add_window(first, bin_row)

        def more(w, c):
            add_window(first + 2 * w, bins[:, at])
            return c

        lax.fori_loop(1, (last - first) // 2 + 1, more, 0)
        return carry

    lax.fori_loop(0, chunks, step, 0)

    def arrange(zb, carry):
        for half in range(2):
            tile = acc[2 * zb + half]
            for quarter in range(4):
                dest = out.at[quarter % 2, zb, quarter // 2]
                dest[half * QUARTER : (half + 1) * QUARTER] = tile[
                    quarter * QUARTER : (quarter + 1) * QUARTER
                ]
        low = acc[2 * zb, 4 * QUARTER : 4 * QUARTER + 8]
        high = acc[2 * zb + 1, 4 * QUARTER : 4 * QUARTER + 8]
        row = lax.broadcasted_iota(jnp.int32, (8, LANES), 0)
        both = jnp.where(row == 0, low, high)
        for quarter in range(4):
            out[quarter % 2, zb, quarter // 2, 2 * QUARTER :] = both
        return carry

    lax.fori_loop(0, tiles // 2, arrange, 0)


def histogram(responses, event_bins, nominal_weight, throws, bins_total):
    events = event_bins.shape[0]
    tiles = bins_total // LANES
    by_chunk = event_bins.reshape(events // CHUNK, CHUNK)
    edges = jnp.stack([by_chunk[:, 0], by_chunk[:, -1]], axis=1)
    vmem = pl.BlockSpec(memory_space=pltpu.VMEM)
    return pl.pallas_call(
        hist_kernel,
        out_shape=jax.ShapeDtypeStruct((2, tiles // 2, 2, BLOCK_ROWS, LANES), F32),
        in_specs=[pl.BlockSpec(memory_space=pltpu.SMEM)] + [vmem] * 4,
        out_specs=vmem,
        scratch_shapes=[
            pltpu.VMEM((tiles + 1, 4 * QUARTER + 16, LANES), F32),
            pltpu.VMEM((4 * QUARTER + 16, CHUNK), jnp.bfloat16),
        ],
        name="histogram",
    )(
        edges,
        responses,
        event_bins.reshape(1, events),
        nominal_weight.astype(F32).reshape(1, events),
        throws.astype(jnp.bfloat16).T,
    )


def exchange_kernel(
    nz, nu, spec_scale, cov_scale,
    part, spectra, cov,
    core_in, summed, x_in, up_in, down_in, up_out, down_out, own, dev, up_blk, down_blk,
    rows_in, cols_in, spec_in, cols_mix, part_out, part_keep, part_in, pack_out, pack_in,
    core_s, core_r, x_s, x_r, up_s, up_r, down_s, down_r,
    gu_s, gu_r, gd_s, gd_r, fwd_s, rows_r, cols_s, cols_r, spec_s, spec_r, tail_s, tail_r,
):
    ev = lax.axis_index("ev")
    u = lax.axis_index("uni")
    z = ev // 4
    xl = lax.rem(ev // 2, 2)
    c = lax.rem(ev, 2)
    core_ev = ev + 1 - 2 * c
    x_ev = ev + 2 - 4 * xl
    diag_ev = x_ev + 1 - 2 * c
    up_ev = lax.rem(ev + 4, 4 * nz)
    down_ev = lax.rem(ev + 4 * nz - 4, 4 * nz)
    half = nz // 2

    def send(src, dst, ssem, rsem, to_ev=ev, to_u=u):
        return pltpu.make_async_remote_copy(
            src_ref=src, dst_ref=dst, send_sem=ssem, recv_sem=rsem,
            device_id={"ev": to_ev, "uni": to_u}, device_id_type=MESH,
        )

    def block_of(k):
        j = (k + 1) // 2
        away = jnp.where(lax.rem(k, 2) == 1, half - j, nz - half + j)
        return lax.rem(z + away, nz)

    barrier = pltpu.get_barrier_semaphore()
    for peer in (core_ev, x_ev, diag_ev, up_ev, down_ev):
        pl.semaphore_signal(barrier, inc=1, device_id={"ev": peer, "uni": u}, device_id_type=MESH)
    for j in range(1, nu):
        pl.semaphore_signal(
            barrier, inc=1, device_id={"ev": ev, "uni": lax.rem(u + j, nu)}, device_id_type=MESH
        )
    pl.semaphore_wait(barrier, 5 + nu - 1)

    def core_copy(k):
        zb = block_of(k)
        return send(part.at[1 - c, zb], core_in.at[zb], core_s.at[k], core_r.at[k], to_ev=core_ev)

    def x_copy(k):
        zb = block_of(k)
        return send(summed.at[zb, 1 - xl], x_in.at[zb], x_s.at[k], x_r.at[k], to_ev=x_ev)

    def start_core(k, carry):
        core_copy(k).start()
        return carry

    lax.fori_loop(0, nz, start_core, 0)

    def start_x(k, carry):
        zb = block_of(k)
        core_copy(k).wait_recv()
        summed[zb] = part[c, zb] + core_in[zb]
        x_copy(k).start()
        return carry

    lax.fori_loop(0, nz, start_x, 0)

    def up_copy(s):
        return send(up_out.at[s], up_in.at[s], up_s.at[s], up_r.at[s], to_ev=up_ev)

    def down_copy(s):
        return send(down_out.at[s], down_in.at[s], down_s.at[s], down_r.at[s], to_ev=down_ev)

    def local_sum(k):
        zb = block_of(k)
        x_copy(k).wait_recv()
        return summed[zb, xl] + x_in[zb]

    up_out[0] = local_sum(0)
    up_copy(0).start()
    down_out[0] = local_sum(2)
    down_copy(0).start()

    def ring_step(s, carry):
        here = local_sum(2 * s - 1)
        up_copy(s - 1).wait_recv()
        up_out[s] = here + up_in[s - 1]
        up_copy(s).start()

        @pl.when(s < half - 1)
        def _():
            here = local_sum(2 * s + 2)
            down_copy(s - 1).wait_recv()
            down_out[s] = here + down_in[s - 1]
            down_copy(s).start()

        return carry

    lax.fori_loop(1, half, ring_step, 0)
    here = local_sum(nz - 1)
    down_copy(half - 2).wait_recv()
    here = here + down_in[half - 2]
    up_copy(half - 1).wait_recv()
    total = here + up_in[half - 1]
    own[...] = total
    dev[:QUARTER] = total[:QUARTER] - total[2 * QUARTER : 2 * QUARTER + 1]
    dev[QUARTER:] = total[QUARTER : 2 * QUARTER] - total[2 * QUARTER + 1 : 2 * QUARTER + 2]

    def gather_up(s, src):
        return send(src, up_blk.at[s], gu_s.at[s], gu_r.at[s], to_ev=up_ev)

    def gather_down(s, src):
        return send(src, down_blk.at[s], gd_s.at[s], gd_r.at[s], to_ev=down_ev)

    def forward(n, src, origin, waiting=False):
        owner = origin // (nz // nu)
        slot = lax.rem(origin, nz // nu)

        @pl.when(owner != u)
        def _():
            copy = send(src, rows_in.at[slot, u], fwd_s.at[n], rows_r.at[slot, u], to_u=owner)
            if waiting:
                copy.wait_send()
            else:
                copy.start()

        if not waiting:

            @pl.when(owner == u)
            def _():
                rows_in[slot, u] = src[...]

    gather_up(0, dev).start()
    gather_down(0, dev).start()

    def cols_copy(j):
        return send(dev, cols_in.at[u], cols_s.at[j], cols_r.at[u], to_u=lax.rem(u + j, nu))

    def start_cols(j, carry):
        cols_copy(j).start()
        return carry

    forward(0, dev, z)
    lax.fori_loop(1, nu, start_cols, 0)
    cols_in[u] = dev[...]

    mine = 2 * xl + c
    spec_peers = ((core_ev, xl), (x_ev, 1 - xl), (diag_ev, 1 - xl))

    def spec_copy(i):
        peer, peer_half = spec_peers[i]
        src = own.at[pl.ds(pl.multiple_of(peer_half * QUARTER, QUARTER), QUARTER)]
        return send(src, spec_in.at[mine], spec_s.at[i], spec_r.at[i], to_ev=peer)

    for i in range(3):
        spec_copy(i).start()
    spec_in[mine] = own[pl.ds(pl.multiple_of(xl * QUARTER, QUARTER), QUARTER)]

    def gather_step(s, carry):
        gather_up(s, dev).wait_recv()

        @pl.when(s < half - 1)
        def _():
            gather_up(s + 1, up_blk.at[s]).start()

        forward(1 + 2 * s, up_blk.at[s], lax.rem(z + nz - 1 - s, nz))

        @pl.when(s < half - 1)
        def _():
            gather_down(s, dev).wait_recv()

            @pl.when(s < half - 2)
            def _():
                gather_down(s + 1, down_blk.at[s]).start()

            forward(2 + 2 * s, down_blk.at[s], lax.rem(z + 1 + s, nz))

        return carry

    lax.fori_loop(0, half, gather_step, 0)

    for i in range(3):
        spec_copy(i).wait_recv()
    by_bin = spec_in[...].reshape(4 * QUARTER, LANES).T
    spectra[...] = jnp.where(c == 0, by_bin[: LANES // 2], by_bin[LANES // 2 :]) * spec_scale

    def wait_cols(j, carry):
        v = lax.rem(u + j, nu)
        send(dev, cols_in.at[v], cols_s.at[j], cols_r.at[v], to_u=v).wait_recv()
        return carry

    lax.fori_loop(1, nu, wait_cols, 0)

    depth = nu * QUARTER
    lane = lax.broadcasted_iota(jnp.int32, (depth, LANES), 1)
    left = cols_in[:, :QUARTER].reshape(depth, LANES)
    right = cols_in[:, QUARTER:].reshape(depth, LANES)
    first = jnp.where(lane < LANES // 2, left, pltpu.roll(right, LANES // 2, 1))
    second = jnp.where(lane < LANES // 2, pltpu.roll(left, LANES // 2, 1), right)
    cols_mix[0] = first
    cols_mix[1] = second

    def wait_rows(j, carry):
        v = lax.rem(u + j, nu)
        for slot in range(nz // nu):
            send(dev, rows_in.at[slot, v], cols_s.at[0], rows_r.at[slot, v], to_u=v).wait_recv()
        return carry

    lax.fori_loop(1, nu, wait_rows, 0)

    def product(which, dest):
        cols = cols_mix[which]
        for slot in range(nz // nu):
            for h in range(2):
                rows = rows_in[slot, :, h * QUARTER : (h + 1) * QUARTER].reshape(depth, LANES)
                at = (2 * slot + h) * LANES
                dest[at : at + LANES] = jnp.dot(
                    rows.T, cols, precision=lax.Precision.HIGHEST, preferred_element_type=F32
                )

    product(1 - c, part_out)
    core_tail = send(part_out, part_in, tail_s.at[0], tail_r.at[0], to_ev=core_ev)
    core_tail.start()
    product(c, part_keep)
    core_tail.wait_recv()
    both = part_keep[...] + part_in[...]
    n_rows = both.shape[0] // 2
    lane = lax.broadcasted_iota(jnp.int32, (n_rows, LANES), 1)
    top, bottom = both[:n_rows], both[n_rows:]
    pack_left = jnp.where(lane < LANES // 2, top, pltpu.roll(bottom, LANES // 2, 1))
    pack_right = jnp.where(lane < LANES // 2, pltpu.roll(top, LANES // 2, 1), bottom)
    pack_out[...] = jnp.where(xl == 0, pack_right, pack_left)
    x_tail = send(pack_out, pack_in, tail_s.at[1], tail_r.at[1], to_ev=x_ev)
    x_tail.start()
    keep = jnp.where(xl == 0, pack_left, pack_right)
    x_tail.wait_recv()
    final = (keep + pack_in[...]) * cov_scale
    cov[:n_rows] = final[:, : LANES // 2]
    cov[n_rows:] = final[:, LANES // 2 :]

    def drain(k, carry):
        core_copy(k).wait_send()
        x_copy(k).wait_send()
        return carry

    lax.fori_loop(0, nz, drain, 0)

    def drain_ring(s, carry):
        up_copy(s).wait_send()
        gather_up(s, dev).wait_send()
        forward(1 + 2 * s, dev, lax.rem(z + nz - 1 - s, nz), waiting=True)

        @pl.when(s < half - 1)
        def _():
            down_copy(s).wait_send()
            gather_down(s, dev).wait_send()
            forward(2 + 2 * s, dev, lax.rem(z + 1 + s, nz), waiting=True)

        return carry

    lax.fori_loop(0, half, drain_ring, 0)
    forward(0, dev, z, waiting=True)

    def drain_cols(j, carry):
        cols_copy(j).wait_send()
        return carry

    lax.fori_loop(1, nu, drain_cols, 0)
    for i in range(3):
        spec_copy(i).wait_send()
    core_tail.wait_send()
    x_tail.wait_send()


def exchange(part, nz, nu, spec_scale, cov_scale):
    half = nz // 2
    rows = nz // nu * 2 * LANES
    block = (BLOCK_ROWS, LANES)
    blk = (2 * QUARTER, LANES)
    vmem = pl.BlockSpec(memory_space=pltpu.VMEM)

    def buf(*shape):
        return pltpu.VMEM(shape, F32)

    def dma(*shape):
        return pltpu.SemaphoreType.DMA(shape)

    return pl.pallas_call(
        functools.partial(exchange_kernel, nz, nu, spec_scale, cov_scale),
        out_shape=(
            jax.ShapeDtypeStruct((LANES // 2, 4 * QUARTER), F32),
            jax.ShapeDtypeStruct((rows, LANES // 2), F32),
        ),
        in_specs=[vmem],
        out_specs=(vmem, vmem),
        scratch_shapes=[
            buf(nz, 2, *block),
            buf(nz, 2, *block),
            buf(nz, *block),
            buf(half, *block), buf(half - 1, *block),
            buf(half, *block), buf(half - 1, *block),
            buf(*block), buf(*blk),
            buf(half, *blk), buf(half - 1, *blk),
            buf(nz // nu, nu, *blk), buf(nu, *blk),
            buf(4, QUARTER, LANES),
            buf(2, nu * QUARTER, LANES),
            buf(rows, LANES), buf(rows, LANES), buf(rows, LANES),
            buf(rows // 2, LANES), buf(rows // 2, LANES),
            dma(nz), dma(nz), dma(nz), dma(nz),
            dma(half), dma(half), dma(half - 1), dma(half - 1),
            dma(half), dma(half), dma(half - 1), dma(half - 1),
            dma(nz), dma(nz // nu, nu), dma(nu), dma(nu),
            dma(3), dma(3), dma(2), dma(2),
        ],
        compiler_params=pltpu.CompilerParams(collective_id=0, has_side_effects=True),
        name="exchange",
    )(part)


def body(responses, event_bins, nominal_weight, throws):
    nz = lax.axis_size("ev") // 4
    nu = lax.axis_size("uni")
    bins_total = nz * 2 * LANES
    per_bin = event_bins.shape[0] * lax.axis_size("ev") // bins_total
    universes = throws.shape[1] * nu
    part = histogram(responses, event_bins, nominal_weight, throws, bins_total)
    return exchange(part, nz, nu, 1.0 / per_bin, 1.0 / (universes * per_bin))


def solution(mesh):
    in_specs = (P(None, "ev"), P("ev"), P("ev"), P(None, "uni"))
    out_specs = (P("ev", "uni"), P("uni", "ev"))
    return jax.shard_map(body, mesh=mesh, in_specs=in_specs, out_specs=out_specs, check_vma=False)
```

```python
import functools

import jax
import jax.numpy as jnp
from jax import lax
from jax.experimental import pallas as pl
from jax.experimental.pallas import tpu as pltpu
from jax.sharding import PartitionSpec as P

LANES = 128
QUARTER = 32
BLOCK_ROWS = 72
CHUNK = 512
VMEM_GRANT = 20 << 20
MESH = pl.DeviceIdType.MESH
F32 = jnp.float32


def hist_kernel(
    resp_hbm, bins_hbm, nominal_hbm, throws_hbm,
    out,
    acc, weights, nominal_rows, resp, bins, nominal, throws, edges, sems,
):
    copies = [
        pltpu.make_async_copy(src, dst, sems.at[i])
        for i, (src, dst) in enumerate(
            [
                (throws_hbm, throws), (bins_hbm, edges), (nominal_hbm, nominal),
                (bins_hbm, bins), (resp_hbm, resp),
            ]
        )
    ]
    for copy in copies:
        copy.start()
    tiles = acc.shape[0] - 1
    chunks = resp.shape[1] // CHUNK
    per_chunk = CHUNK // LANES
    zero_tile = jnp.zeros(acc.shape[1:], F32)

    def clear(t, carry):
        acc[t] = zero_tile
        return carry

    lax.fori_loop(0, tiles + 1, clear, 0)
    for copy in copies:
        copy.wait()
    nominal_rows[...] = nominal[...].astype(F32)
    knob_throws = throws[...].astype(F32).T.astype(jnp.bfloat16)
    bin_iota = lax.broadcasted_iota(jnp.int32, (2 * LANES, CHUNK), 0)

    def row_of(ref, i):
        return jnp.concatenate(
            [ref[pl.ds(i * per_chunk + g, 1), :] for g in range(per_chunk)], axis=1
        )

    def first_tile(i):
        return edges[i * per_chunk, 0] // LANES

    def weigh(i, slot):
        at = pl.ds(pl.multiple_of(i * CHUNK, CHUNK), CHUNK)
        nominal_row = row_of(nominal_rows, i)
        log_weight = jnp.dot(knob_throws, resp[:, at], preferred_element_type=F32)
        weights[slot, : 4 * QUARTER] = (nominal_row * jnp.exp(log_weight)).astype(jnp.bfloat16)
        weights[slot, 4 * QUARTER :] = jnp.broadcast_to(nominal_row, (16, CHUNK)).astype(
            jnp.bfloat16
        )

    def add_window(i, slot, tile):
        local = row_of(bins, i) - tile * LANES
        onehot = jnp.where(bin_iota == local, 1.0, 0.0).astype(jnp.bfloat16)
        part = lax.dot_general(
            weights[slot], onehot, (((1,), (1,)), ((), ())), preferred_element_type=F32
        )
        low, high = acc[tile] + part[:, :LANES], acc[tile + 1] + part[:, LANES:]
        acc[tile] = low
        acc[tile + 1] = high

    def add_rest(i, slot):
        first = first_tile(i)
        last = edges[i * per_chunk + per_chunk - 1, LANES - 1] // LANES

        def more(w, c):
            add_window(i, slot, first + 2 * w)
            return c

        lax.fori_loop(1, (last - first) // 2 + 1, more, 0)

    weigh(0, 0)

    def step(j, carry):
        weigh(2 * j + 1, 1)
        add_window(2 * j, 0, first_tile(2 * j))
        add_rest(2 * j, 0)
        weigh(jnp.minimum(2 * j + 2, chunks - 1), 0)
        add_window(2 * j + 1, 1, first_tile(2 * j + 1))
        add_rest(2 * j + 1, 1)
        return carry

    lax.fori_loop(0, chunks // 2, step, 0)

    def arrange(zb, carry):
        for half in range(2):
            tile = acc[2 * zb + half]
            for quarter in range(4):
                dest = out.at[quarter % 2, zb, quarter // 2]
                dest[half * QUARTER : (half + 1) * QUARTER] = tile[
                    quarter * QUARTER : (quarter + 1) * QUARTER
                ]
        low = acc[2 * zb, 4 * QUARTER : 4 * QUARTER + 8]
        high = acc[2 * zb + 1, 4 * QUARTER : 4 * QUARTER + 8]
        row = lax.broadcasted_iota(jnp.int32, (8, LANES), 0)
        both = jnp.where(row == 0, low, high)
        for quarter in range(4):
            out[quarter % 2, zb, quarter // 2, 2 * QUARTER :] = both
        return carry

    lax.fori_loop(0, tiles // 2, arrange, 0)


def histogram(responses, event_bins, nominal_weight, throws, bins_total):
    events = event_bins.shape[0]
    tiles = bins_total // LANES
    bins = event_bins.reshape(events // LANES, LANES)
    vmem = pl.BlockSpec(memory_space=pltpu.VMEM)
    return pl.pallas_call(
        hist_kernel,
        out_shape=jax.ShapeDtypeStruct((2, tiles // 2, 2, BLOCK_ROWS, LANES), F32),
        in_specs=[pl.BlockSpec(memory_space=pltpu.HBM)] * 4,
        out_specs=vmem,
        scratch_shapes=[
            pltpu.VMEM((tiles + 1, 4 * QUARTER + 16, LANES), F32),
            pltpu.VMEM((2, 4 * QUARTER + 16, CHUNK), jnp.bfloat16),
            pltpu.VMEM((events // LANES, LANES), F32),
            pltpu.VMEM(responses.shape, responses.dtype),
            pltpu.VMEM((events // LANES, LANES), jnp.int32),
            pltpu.VMEM((events // LANES, LANES), nominal_weight.dtype),
            pltpu.VMEM(throws.shape, throws.dtype),
            pltpu.SMEM((events // LANES, LANES), jnp.int32),
            pltpu.SemaphoreType.DMA((5,)),
        ],
        compiler_params=pltpu.CompilerParams(vmem_limit_bytes=VMEM_GRANT),
        name="histogram",
    )(*[pltpu.with_memory_space_constraint(x, pltpu.HBM) for x in (responses, bins, nominal_weight.reshape(events // LANES, LANES), throws)])


def exchange_kernel(
    nz, nu, spec_scale, cov_scale,
    part, spectra, cov,
    core_in, summed, x_in, ring_out, ring_in, own, dev, blocks,
    rows_in, cols_in, spec_in, prod, prod_in, pack_out, pack_in,
    core_s, core_r, x_s, x_r, ring_s, ring_r,
    blk_s, blk_r, fwd_s, rows_r, cols_s, cols_r, spec_s, spec_r, tail_s, tail_r,
):
    ev = lax.axis_index("ev")
    u = lax.axis_index("uni")
    z = ev // 4
    xl = lax.rem(ev // 2, 2)
    c = lax.rem(ev, 2)
    core_ev = ev + 1 - 2 * c
    x_ev = ev + 2 - 4 * xl
    diag_ev = x_ev + 1 - 2 * c
    half = nz // 2
    sum_skip = half // 2
    blk_skip = half // 2 + 1
    slots = nz // nu

    def along(d):
        return lax.rem(ev + 4 * (d % nz), 4 * nz)

    def z_at(d):
        return lax.rem(z + d % nz, nz)

    def send(src, dst, ssem, rsem, to_ev=ev, to_u=u):
        return pltpu.make_async_remote_copy(
            src_ref=src, dst_ref=dst, send_sem=ssem, recv_sem=rsem,
            device_id={"ev": to_ev, "uni": to_u}, device_id_type=MESH,
        )

    def block_of(k):
        j = (k + 1) // 2
        away = jnp.where(lax.rem(k, 2) == 1, half - j, nz - half + j)
        return lax.rem(z + away, nz)

    barrier = pltpu.get_barrier_semaphore()
    peers = [core_ev, x_ev, diag_ev]
    for d in sorted({1, sum_skip, blk_skip}):
        peers += [along(d), along(-d)]
    for peer in peers:
        pl.semaphore_signal(barrier, inc=1, device_id={"ev": peer, "uni": u}, device_id_type=MESH)
    for j in range(1, nu):
        pl.semaphore_signal(
            barrier, inc=1, device_id={"ev": ev, "uni": lax.rem(u + j, nu)}, device_id_type=MESH
        )
    pl.semaphore_wait(barrier, len(peers) + nu - 1)

    def core_copy(k):
        zb = block_of(k)
        return send(part.at[1 - c, zb], core_in.at[zb], core_s.at[k], core_r.at[k], to_ev=core_ev)

    def x_copy(k):
        zb = block_of(k)
        return send(summed.at[zb, 1 - xl], x_in.at[zb], x_s.at[k], x_r.at[k], to_ev=x_ev)

    def start_core(k, carry):
        core_copy(k).start()
        return carry

    lax.fori_loop(0, nz, start_core, 0)

    def start_x(k, carry):
        zb = block_of(k)
        core_copy(k).wait_recv()
        summed[zb] = part[c, zb] + core_in[zb]
        x_copy(k).start()
        return carry

    lax.fori_loop(0, nz, start_x, 0)

    sends = []
    arrivals = {}

    def ring_copy(n, way, to):
        return send(ring_out.at[n], ring_in.at[n], ring_s.at[n], ring_r.at[n], to_ev=along(way * to))

    def sum_step(way, d, first, to):
        n = len(sends)
        k = 0 if d == half else 2 * (half - d) - (way > 0)
        x_copy(k).wait_recv()
        zb = z_at(way * d)
        value = summed[zb, xl] + x_in[zb]
        if not first:
            slot, before = arrivals[way, d + 1]
            before.wait_recv()
            value = value + ring_in[slot]
        ring_out[n] = value
        copy = ring_copy(n, way, to)
        copy.start()
        sends.append(copy)
        arrivals[way, d] = n, copy

    order = []
    for d in range(half, sum_skip - 1, -1):
        for way in (1, -1):
            if way * d > -half:
                first = d == half or (way < 0 and d == half - 1)
                order.append((way, d, first, sum_skip if d == sum_skip else 1))
    near = [(way, d, d == sum_skip - 1, 1) for d in range(sum_skip - 1, 0, -1) for way in (1, -1)]
    order = order[:-2] + near[:2] + order[-2:] + near[2:]
    for step in order:
        sum_step(*step)
    x_copy(nz - 1).wait_recv()
    total = summed[z, xl] + x_in[z]
    finals = [arrivals[way, sum_skip] for way in (1, -1)]
    if sum_skip > 1:
        finals += [arrivals[way, 1] for way in (1, -1)]
    for slot, copy in finals:
        copy.wait_recv()
        total = total + ring_in[slot]
    own[...] = total
    dev[:QUARTER] = total[:QUARTER] - total[2 * QUARTER : 2 * QUARTER + 1]
    dev[QUARTER:] = total[QUARTER : 2 * QUARTER] - total[2 * QUARTER + 1 : 2 * QUARTER + 2]

    slot_of = {}
    blk_sends = []

    def block_copy(src, way, d, to):
        n = slot_of.setdefault((way, d), len(slot_of))
        copy = send(src, blocks.at[n], blk_s.at[n], blk_r.at[n], to_ev=along(way * to))
        copy.start()
        blk_sends.append(copy)

    def forward(n, src, origin, waiting=False):
        owner = origin // slots
        slot = lax.rem(origin, slots)

        @pl.when(owner != u)
        def _():
            copy = send(src, rows_in.at[slot, u], fwd_s.at[n], rows_r.at[slot, u], to_u=owner)
            if waiting:
                copy.wait_send()
            else:
                copy.start()

        if not waiting:

            @pl.when(owner == u)
            def _():
                rows_in[slot, u] = src[...]

    reach = {1: half, -1: half - 1}
    for way in (1, -1):
        if blk_skip <= reach[way]:
            block_copy(dev, way, blk_skip, blk_skip)
    for way in (1, -1):
        block_copy(dev, way, 1, 1)

    def cols_copy(j):
        return send(dev, cols_in.at[u], cols_s.at[j], cols_r.at[u], to_u=lax.rem(u + j, nu))

    def start_cols(j, carry):
        cols_copy(j).start()
        return carry

    lax.fori_loop(1, nu, start_cols, 0)
    forward(0, dev, z)
    cols_in[u] = dev[...]

    mine = 2 * xl + c
    spec_peers = ((core_ev, xl), (x_ev, 1 - xl), (diag_ev, 1 - xl))

    def spec_copy(i):
        peer, peer_half = spec_peers[i]
        src = own.at[pl.ds(pl.multiple_of(peer_half * QUARTER, QUARTER), QUARTER)]
        return send(src, spec_in.at[mine], spec_s.at[i], spec_r.at[i], to_ev=peer)

    for i in range(3):
        spec_copy(i).start()
    spec_in[mine] = own[pl.ds(pl.multiple_of(xl * QUARTER, QUARTER), QUARTER)]

    forwards = []

    def block_step(way, d):
        n = slot_of[way, d]
        send(dev, blocks.at[n], blk_s.at[n], blk_r.at[n], to_ev=along(way)).wait_recv()
        if d + 1 <= reach[way] and d + 1 != blk_skip:
            block_copy(blocks.at[n], way, d + 1, 1)
        forwards.append((blocks.at[n], z_at(-way * d)))
        forward(len(forwards), *forwards[-1])

    near = list(range(1, blk_skip))
    far = list(range(blk_skip, half + 1))
    order = near[:2]
    for i in range(max(len(far), len(near) - 2)):
        order += far[i : i + 1] + near[i + 2 : i + 3]
    for d in order:
        for way in (1, -1):
            if d <= reach[way]:
                block_step(way, d)

    for i in range(3):
        spec_copy(i).wait_recv()
    by_bin = spec_in[...].reshape(4 * QUARTER, LANES).T
    spectra[...] = jnp.where(c == 0, by_bin[: LANES // 2], by_bin[LANES // 2 :]) * spec_scale

    def wait_cols(j, carry):
        v = lax.rem(u + j, nu)
        send(dev, cols_in.at[v], cols_s.at[j], cols_r.at[v], to_u=v).wait_recv()
        return carry

    lax.fori_loop(1, nu, wait_cols, 0)

    depth = nu * QUARTER
    bf16 = jnp.bfloat16
    lane = lax.broadcasted_iota(jnp.int32, (depth, LANES), 1)
    left = cols_in[:, :QUARTER].reshape(depth, LANES)
    right = cols_in[:, QUARTER:].reshape(depth, LANES)
    cols = jnp.concatenate(
        [
            jnp.where(lane < LANES // 2, left, pltpu.roll(right, LANES // 2, 1)).T,
            jnp.where(lane < LANES // 2, pltpu.roll(left, LANES // 2, 1), right).T,
        ],
        axis=0,
    )
    cols_hi = cols.astype(bf16)
    cols_lo = (cols - cols_hi.astype(F32)).astype(bf16)
    cols_all = jnp.concatenate([cols_hi, cols_hi, cols_lo], axis=1)
    xl_rows = pl.ds(pl.multiple_of((1 - xl) * (LANES // 2), LANES // 2), LANES // 2)
    my_rows = pl.ds(pl.multiple_of(xl * (LANES // 2), LANES // 2), LANES // 2)

    def core_tail(slot):
        return send(
            prod.at[slot, 1 - c], prod_in.at[slot], tail_s.at[0, slot], tail_r.at[0, slot],
            to_ev=core_ev,
        )

    def x_tail(slot):
        return send(
            pack_out.at[slot], pack_in.at[slot], tail_s.at[1, slot], tail_r.at[1, slot], to_ev=x_ev
        )

    for slot in range(slots):

        def wait_rows(j, carry, slot=slot):
            v = lax.rem(u + j, nu)
            send(dev, rows_in.at[slot, v], cols_s.at[0], rows_r.at[slot, v], to_u=v).wait_recv()
            return carry

        lax.fori_loop(1, nu, wait_rows, 0)
        rows = jnp.concatenate(
            [
                rows_in[slot, :, :QUARTER].reshape(depth, LANES),
                rows_in[slot, :, QUARTER:].reshape(depth, LANES),
            ],
            axis=1,
        )
        rows_hi = rows.astype(bf16)
        rows_lo = (rows - rows_hi.astype(F32)).astype(bf16)
        rows_all = jnp.concatenate([rows_hi, rows_lo, rows_hi], axis=0)
        product = jnp.dot(cols_all, rows_all, preferred_element_type=F32)
        prod[slot, 0] = product[:LANES]
        prod[slot, 1] = product[LANES:]
        core_tail(slot).start()
    for slot in range(slots):
        core_tail(slot).wait_recv()
        pack_out[slot] = prod[slot, c, xl_rows] + prod_in[slot, xl_rows]
        x_tail(slot).start()
    for slot in range(slots):
        x_tail(slot).wait_recv()
        keep = prod[slot, c, my_rows] + prod_in[slot, my_rows]
        cov[:, slot * 2 * LANES : (slot + 1) * 2 * LANES] = (keep + pack_in[slot]) * cov_scale

    def drain(k, carry):
        core_copy(k).wait_send()
        x_copy(k).wait_send()
        return carry

    lax.fori_loop(0, nz, drain, 0)
    for copy in sends + blk_sends:
        copy.wait_send()
    forward(0, dev, z, waiting=True)
    for n, (src, origin) in enumerate(forwards):
        forward(n + 1, src, origin, waiting=True)

    def drain_cols(j, carry):
        cols_copy(j).wait_send()
        return carry

    lax.fori_loop(1, nu, drain_cols, 0)
    for i in range(3):
        spec_copy(i).wait_send()
    for slot in range(slots):
        core_tail(slot).wait_send()
        x_tail(slot).wait_send()


def exchange(part, nz, nu, spec_scale, cov_scale):
    slots = nz // nu
    rows = slots * 2 * LANES
    block = (BLOCK_ROWS, LANES)
    blk = (2 * QUARTER, LANES)
    vmem = pl.BlockSpec(memory_space=pltpu.VMEM)

    def buf(*shape):
        return pltpu.VMEM(shape, F32)

    def dma(*shape):
        return pltpu.SemaphoreType.DMA(shape)

    spectra, cov = pl.pallas_call(
        functools.partial(exchange_kernel, nz, nu, spec_scale, cov_scale),
        out_shape=(
            jax.ShapeDtypeStruct((LANES // 2, 4 * QUARTER), F32),
            jax.ShapeDtypeStruct((LANES // 2, rows), F32),
        ),
        in_specs=[vmem],
        out_specs=(vmem, vmem),
        scratch_shapes=[
            buf(nz, 2, *block),
            buf(nz, 2, *block),
            buf(nz, *block),
            buf(nz - 1, *block), buf(nz - 1, *block),
            buf(*block), buf(*blk),
            buf(nz - 1, *blk),
            buf(slots, nu, *blk), buf(nu, *blk),
            buf(4, QUARTER, LANES),
            buf(slots, 2, LANES, 2 * LANES), buf(slots, LANES, 2 * LANES),
            buf(slots, LANES // 2, 2 * LANES), buf(slots, LANES // 2, 2 * LANES),
            dma(nz), dma(nz), dma(nz), dma(nz),
            dma(nz - 1), dma(nz - 1),
            dma(nz - 1), dma(nz - 1),
            dma(nz), dma(slots, nu), dma(nu), dma(nu),
            dma(3), dma(3), dma(2, slots), dma(2, slots),
        ],
        compiler_params=pltpu.CompilerParams(
            collective_id=0, has_side_effects=True, vmem_limit_bytes=VMEM_GRANT
        ),
        name="exchange",
    )(part)
    return spectra, cov.T


def body(responses, event_bins, nominal_weight, throws):
    nz = lax.axis_size("ev") // 4
    nu = lax.axis_size("uni")
    bins_total = nz * 2 * LANES
    per_bin = event_bins.shape[0] * lax.axis_size("ev") // bins_total
    universes = throws.shape[1] * nu
    part = histogram(responses, event_bins, nominal_weight, throws, bins_total)
    return exchange(part, nz, nu, 1.0 / per_bin, 1.0 / (universes * per_bin))


def solution(mesh):
    in_specs = (P(None, "ev"), P("ev"), P("ev"), P(None, "uni"))
    out_specs = (P("ev", "uni"), P("uni", "ev"))
    return jax.shard_map(body, mesh=mesh, in_specs=in_specs, out_specs=out_specs, check_vma=False)
```

```python
import functools

import jax
import jax.numpy as jnp
from jax import lax
from jax.experimental import pallas as pl
from jax.experimental.pallas import tpu as pltpu
from jax.sharding import PartitionSpec as P

LANES = 128
QUARTER = 32
BLOCK_ROWS = 72
CHUNK = 512
WINDOW = 1280
LAG = 7
VMEM_GRANT = 20 << 20
MESH = pl.DeviceIdType.MESH
F32 = jnp.float32


def block_histogram(weights, local):
    iota = lax.broadcasted_iota(jnp.int32, (2 * LANES, local.shape[1]), 0)
    onehot = jnp.where(iota == local, 1.0, 0.0).astype(jnp.bfloat16)
    return lax.dot_general(
        weights, onehot, (((1,), (1,)), ((), ())), preferred_element_type=F32
    )


def weigh(knob_throws, resp, nominal_row):
    log_weight = jnp.dot(knob_throws, resp, preferred_element_type=F32)
    return (nominal_row * jnp.exp(log_weight)).astype(jnp.bfloat16)


def central_rows(nominal_row):
    return jnp.broadcast_to(nominal_row, (16, nominal_row.shape[1])).astype(jnp.bfloat16)


def rows_of(ref, start, count):
    return jnp.concatenate([ref[pl.ds(start + g, 1), :] for g in range(count)], axis=1)


def quarter_blocks(sums):
    row = lax.broadcasted_iota(jnp.int32, (8, LANES), 0)
    tail = sums[4 * QUARTER : 4 * QUARTER + 8]
    central = jnp.where(row == 0, tail[:, :LANES], tail[:, LANES:])
    for quarter in range(4):
        mine = sums[quarter * QUARTER : (quarter + 1) * QUARTER]
        block = jnp.concatenate([mine[:, :LANES], mine[:, LANES:], central], axis=0)
        yield quarter % 2, quarter // 2, block


def windows_kernel(
    resp_hbm, bins_hbm, nominal_hbm, throws_hbm,
    resp_of, local_of, nominal_of, throws_t, extra,
    resp, bins, nominal, throws, nominal_rows, acc, starts, sems, resp_sems,
):
    nz = resp_of.shape[0]
    per_row = LANES
    rows = bins_hbm.shape[0]
    window = WINDOW // LANES
    loads = [
        pltpu.make_async_copy(src, dst, sems.at[i])
        for i, (src, dst) in enumerate(
            [(bins_hbm, bins), (nominal_hbm, nominal), (throws_hbm, throws)]
        )
    ]
    for load in loads:
        load.start()

    def clear(zb, carry):
        extra[:, zb] = jnp.zeros((2, 2, BLOCK_ROWS, LANES), F32)
        return carry

    lax.fori_loop(0, nz, clear, 0)
    for load in loads:
        load.wait()
    all_bins = bins[...]
    below = [jnp.int32(0)]
    for zb in range(1, nz):
        hits = jnp.sum(jnp.where(all_bins < zb * 2 * LANES, 1.0, 0.0), axis=0, keepdims=True)
        below.append(jnp.sum(hits).astype(jnp.int32))
    below.append(jnp.int32(rows * LANES))
    beyond = jnp.int32(0)
    for zb in range(nz):
        start = jnp.minimum(below[zb] // LANES, rows - window)
        starts[zb] = start
        beyond = jnp.maximum(beyond, below[zb + 1] - (start + window) * LANES)

    def resp_copy(zb):
        events = pl.ds(pl.multiple_of(starts[zb] * LANES, LANES), WINDOW)
        return pltpu.make_async_copy(resp_hbm.at[:, events], resp_of.at[zb], resp_sems.at[zb])

    def start_copy(zb, carry):
        resp_copy(zb).start()
        return carry

    lax.fori_loop(0, nz, start_copy, 0)
    nominal_rows[...] = nominal[...].astype(F32)
    knob_throws = throws[...].astype(F32).T.astype(jnp.bfloat16)
    throws_t[...] = knob_throws

    def take(zb, carry):
        at = starts[zb]
        for g in range(window):
            lanes = slice(g * LANES, (g + 1) * LANES)
            local_of[zb, :, lanes] = bins[pl.ds(at + g, 1), :] - zb * 2 * LANES
            nominal_of[zb, :, lanes] = nominal_rows[pl.ds(at + g, 1), :]
        return carry

    lax.fori_loop(0, nz, take, 0)

    @pl.when(beyond > 0)
    def _():
        copy = pltpu.make_async_copy(resp_hbm, resp, sems.at[3])
        copy.start()
        copy.wait()
        count = CHUNK // LANES

        def one_block(zb, carry):
            acc[...] = jnp.zeros(acc.shape, F32)
            first = starts[zb] + window

            def one_chunk(row, c):
                at = jnp.minimum(row, rows - count)
                nominal_row = rows_of(nominal_rows, at, count)
                events = pl.ds(pl.multiple_of(at * LANES, LANES), CHUNK)
                index = at * LANES + lax.broadcasted_iota(jnp.int32, (1, CHUNK), 1)
                bin_row = jnp.where(index >= row * LANES, rows_of(bins, at, count), -1)
                all_weights = jnp.concatenate(
                    [weigh(knob_throws, resp[:, events], nominal_row), central_rows(nominal_row)],
                    axis=0,
                )
                acc[...] += block_histogram(all_weights, bin_row - zb * 2 * LANES)
                return c

            def step(i, c):
                row = first + i * count

                @pl.when(row < rows)
                def _():
                    @pl.when(bins_row_min(bins, row) < (zb + 1) * 2 * LANES)
                    def _():
                        one_chunk(row, 0)

                return c

            lax.fori_loop(0, rows // count, step, 0)
            for c, x, block in quarter_blocks(acc[...]):
                extra[c, zb, x] = block
            return carry

        lax.fori_loop(0, nz, one_block, 0)

    def wait_copy(zb, carry):
        resp_copy(zb).wait()
        return carry

    lax.fori_loop(0, nz, wait_copy, 0)


def bins_row_min(bins, row):
    return jnp.min(bins[pl.ds(row, 1), :])


def windows(responses, bins, nominal, throws, nz):
    rows = bins.shape[0]
    hbm = pl.BlockSpec(memory_space=pltpu.HBM)
    vmem = pl.BlockSpec(memory_space=pltpu.VMEM)
    shape = jax.ShapeDtypeStruct
    return pl.pallas_call(
        windows_kernel,
        out_shape=(
            shape((nz, responses.shape[0], WINDOW), responses.dtype),
            shape((nz, 1, WINDOW), jnp.int32),
            shape((nz, 1, WINDOW), F32),
            shape(throws.shape[::-1], jnp.bfloat16),
            shape((2, nz, 2, BLOCK_ROWS, LANES), F32),
        ),
        in_specs=[hbm] * 4,
        out_specs=(vmem,) * 5,
        scratch_shapes=[
            pltpu.VMEM(responses.shape, responses.dtype),
            pltpu.VMEM(bins.shape, jnp.int32),
            pltpu.VMEM(nominal.shape, nominal.dtype),
            pltpu.VMEM(throws.shape, throws.dtype),
            pltpu.VMEM((rows, LANES), F32),
            pltpu.VMEM((4 * QUARTER + 16, 2 * LANES), F32),
            pltpu.SMEM((nz,), jnp.int32),
            pltpu.SemaphoreType.DMA((4,)),
            pltpu.SemaphoreType.DMA((nz,)),
        ],
        compiler_params=pltpu.CompilerParams(vmem_limit_bytes=VMEM_GRANT),
        name="windows",
    )(responses, bins, nominal, throws)


def exchange_kernel(
    nz, nu, spec_scale, cov_scale,
    resp_of, local_of, nominal_of, throws_t, extra,
    spectra, cov,
    part,
    core_in, summed, x_in, ring_out, ring_in, own, dev, blocks,
    rows_in, cols_in, spec_in, prod, prod_in, pack_out, pack_in,
    core_s, core_r, x_s, x_r, ring_s, ring_r,
    blk_s, blk_r, fwd_s, rows_r, cols_s, cols_r, spec_s, spec_r, tail_s, tail_r,
):
    ev = lax.axis_index("ev")
    u = lax.axis_index("uni")
    z = ev // 4
    xl = lax.rem(ev // 2, 2)
    c = lax.rem(ev, 2)
    core_ev = ev + 1 - 2 * c
    x_ev = ev + 2 - 4 * xl
    diag_ev = x_ev + 1 - 2 * c
    half = nz // 2
    sum_skip = half // 2
    blk_skip = half // 2 + 1
    slots = nz // nu

    def along(d):
        return lax.rem(ev + 4 * (d % nz), 4 * nz)

    def z_at(d):
        return lax.rem(z + d % nz, nz)

    def send(src, dst, ssem, rsem, to_ev=ev, to_u=u):
        return pltpu.make_async_remote_copy(
            src_ref=src, dst_ref=dst, send_sem=ssem, recv_sem=rsem,
            device_id={"ev": to_ev, "uni": to_u}, device_id_type=MESH,
        )

    def block_of(k):
        j = (k + 1) // 2
        away = jnp.where(lax.rem(k, 2) == 1, half - j, nz - half + j)
        return lax.rem(z + away, nz)

    barrier = pltpu.get_barrier_semaphore()
    peers = [core_ev, x_ev, diag_ev]
    for d in sorted({1, sum_skip, blk_skip}):
        peers += [along(d), along(-d)]
    for peer in peers:
        pl.semaphore_signal(barrier, inc=1, device_id={"ev": peer, "uni": u}, device_id_type=MESH)
    for j in range(1, nu):
        pl.semaphore_signal(
            barrier, inc=1, device_id={"ev": ev, "uni": lax.rem(u + j, nu)}, device_id_type=MESH
        )
    knob_throws = throws_t[...]
    pl.semaphore_wait(barrier, len(peers) + nu - 1)

    def core_copy(k):
        zb = block_of(k)
        return send(part.at[1 - c, zb], core_in.at[zb], core_s.at[k], core_r.at[k], to_ev=core_ev)

    def x_copy(k):
        zb = block_of(k)
        return send(summed.at[zb, 1 - xl], x_in.at[zb], x_s.at[k], x_r.at[k], to_ev=x_ev)

    def histogram(k):
        zb = block_of(k)
        nominal_row = nominal_of[zb]
        weights = jnp.concatenate(
            [weigh(knob_throws, resp_of[zb], nominal_row), central_rows(nominal_row)], axis=0
        )
        sums = block_histogram(weights, local_of[zb])
        for to_core, to_x, block in quarter_blocks(sums):
            part[to_core, zb, to_x] = block + extra[to_core, zb, to_x]
        core_copy(k).start()

    def start_x(k):
        zb = block_of(k)
        core_copy(k).wait_recv()
        summed[zb] = part[c, zb] + core_in[zb]
        x_copy(k).start()

    def ring_copy(k):
        way = jnp.where((lax.rem(k, 2) == 1) | (k == 0), 1, -1)
        to = jnp.where(half - (k + 1) // 2 == sum_skip, sum_skip, 1)
        to_ev = lax.rem(ev + 4 * (nz + way * to), 4 * nz)
        return send(ring_out.at[k], ring_in.at[k], ring_s.at[k], ring_r.at[k], to_ev=to_ev)

    def sum_step(k):
        zb = block_of(k)
        x_copy(k).wait_recv()
        value = summed[zb, xl] + x_in[zb]
        starts_chain = (k == 0) | (k == 2) | (half - (k + 1) // 2 == sum_skip - 1)

        @pl.when(starts_chain)
        def _():
            ring_out[k] = value

        @pl.when(jnp.logical_not(starts_chain))
        def _():
            before = jnp.maximum(k - 2, 0)
            ring_copy(before).wait_recv()
            ring_out[k] = value + ring_in[before]

        ring_copy(k).start()

    def block_step_of(k, carry):
        @pl.when(k < nz)
        def _():
            histogram(k)

        @pl.when((k > 0) & (k <= nz))
        def _():
            start_x(k - 1)

        @pl.when(k >= LAG)
        def _():
            sum_step(k - LAG)

        return carry

    lax.fori_loop(0, nz - 1 + LAG, block_step_of, 0)
    x_copy(nz - 1).wait_recv()
    total = summed[z, xl] + x_in[z]
    last_far = 2 * (half - sum_skip)
    for k in sorted({last_far - 1, last_far, nz - 3, nz - 2}):
        ring_copy(k).wait_recv()
        total = total + ring_in[k]
    own[...] = total
    dev[:QUARTER] = total[:QUARTER] - total[2 * QUARTER : 2 * QUARTER + 1]
    dev[QUARTER:] = total[QUARTER : 2 * QUARTER] - total[2 * QUARTER + 1 : 2 * QUARTER + 2]

    slot_of = {}
    blk_sends = []

    def block_copy(src, way, d, to):
        n = slot_of.setdefault((way, d), len(slot_of))
        copy = send(src, blocks.at[n], blk_s.at[n], blk_r.at[n], to_ev=along(way * to))
        copy.start()
        blk_sends.append(copy)

    def forward(n, src, origin, waiting=False):
        owner = origin // slots
        slot = lax.rem(origin, slots)

        @pl.when(owner != u)
        def _():
            copy = send(src, rows_in.at[slot, u], fwd_s.at[n], rows_r.at[slot, u], to_u=owner)
            if waiting:
                copy.wait_send()
            else:
                copy.start()

        if not waiting:

            @pl.when(owner == u)
            def _():
                rows_in[slot, u] = src[...]

    reach = {1: half, -1: half - 1}
    for way in (1, -1):
        if blk_skip <= reach[way]:
            block_copy(dev, way, blk_skip, blk_skip)
    for way in (1, -1):
        block_copy(dev, way, 1, 1)

    def cols_copy(j):
        return send(dev, cols_in.at[u], cols_s.at[j], cols_r.at[u], to_u=lax.rem(u + j, nu))

    def start_cols(j, carry):
        cols_copy(j).start()
        return carry

    lax.fori_loop(1, nu, start_cols, 0)
    forward(0, dev, z)
    cols_in[u] = dev[...]

    mine = 2 * xl + c
    spec_peers = ((core_ev, xl), (x_ev, 1 - xl), (diag_ev, 1 - xl))

    def spec_copy(i):
        peer, peer_half = spec_peers[i]
        src = own.at[pl.ds(pl.multiple_of(peer_half * QUARTER, QUARTER), QUARTER)]
        return send(src, spec_in.at[mine], spec_s.at[i], spec_r.at[i], to_ev=peer)

    for i in range(3):
        spec_copy(i).start()
    spec_in[mine] = own[pl.ds(pl.multiple_of(xl * QUARTER, QUARTER), QUARTER)]

    forwards = []

    def block_step(way, d):
        n = slot_of[way, d]
        send(dev, blocks.at[n], blk_s.at[n], blk_r.at[n], to_ev=along(way)).wait_recv()
        if d + 1 <= reach[way] and d + 1 != blk_skip:
            block_copy(blocks.at[n], way, d + 1, 1)
        forwards.append((blocks.at[n], z_at(-way * d)))
        forward(len(forwards), *forwards[-1])

    near = list(range(1, blk_skip))
    far = list(range(blk_skip, half + 1))
    order = near[:1]
    for i in range(max(len(far), len(near) - 1)):
        order += far[i : i + 1] + near[i + 1 : i + 2]
    for d in order:
        for way in (1, -1):
            if d <= reach[way]:
                block_step(way, d)

    for i in range(3):
        spec_copy(i).wait_recv()
    by_bin = spec_in[...].reshape(4 * QUARTER, LANES).T
    spectra[...] = jnp.where(c == 0, by_bin[: LANES // 2], by_bin[LANES // 2 :]) * spec_scale

    def wait_cols(j, carry):
        v = lax.rem(u + j, nu)
        send(dev, cols_in.at[v], cols_s.at[j], cols_r.at[v], to_u=v).wait_recv()
        return carry

    lax.fori_loop(1, nu, wait_cols, 0)

    depth = nu * QUARTER
    bf16 = jnp.bfloat16
    lane = lax.broadcasted_iota(jnp.int32, (depth, LANES), 1)
    left = cols_in[:, :QUARTER].reshape(depth, LANES)
    right = cols_in[:, QUARTER:].reshape(depth, LANES)
    cols = jnp.concatenate(
        [
            jnp.where(lane < LANES // 2, left, pltpu.roll(right, LANES // 2, 1)).T,
            jnp.where(lane < LANES // 2, pltpu.roll(left, LANES // 2, 1), right).T,
        ],
        axis=0,
    )
    cols_hi = cols.astype(bf16)
    cols_lo = (cols - cols_hi.astype(F32)).astype(bf16)
    cols_all = jnp.concatenate([cols_hi, cols_hi, cols_lo], axis=1)
    xl_rows = pl.ds(pl.multiple_of((1 - xl) * (LANES // 2), LANES // 2), LANES // 2)
    my_rows = pl.ds(pl.multiple_of(xl * (LANES // 2), LANES // 2), LANES // 2)

    def core_tail(slot):
        return send(
            prod.at[slot, 1 - c], prod_in.at[slot], tail_s.at[0, slot], tail_r.at[0, slot],
            to_ev=core_ev,
        )

    def x_tail(slot):
        return send(
            pack_out.at[slot], pack_in.at[slot], tail_s.at[1, slot], tail_r.at[1, slot], to_ev=x_ev
        )

    for slot in range(slots):

        def wait_rows(j, carry, slot=slot):
            v = lax.rem(u + j, nu)
            send(dev, rows_in.at[slot, v], cols_s.at[0], rows_r.at[slot, v], to_u=v).wait_recv()
            return carry

        lax.fori_loop(1, nu, wait_rows, 0)
        rows = jnp.concatenate(
            [
                rows_in[slot, :, :QUARTER].reshape(depth, LANES),
                rows_in[slot, :, QUARTER:].reshape(depth, LANES),
            ],
            axis=1,
        )
        rows_hi = rows.astype(bf16)
        rows_lo = (rows - rows_hi.astype(F32)).astype(bf16)
        rows_all = jnp.concatenate([rows_hi, rows_lo, rows_hi], axis=0)
        product = jnp.dot(cols_all, rows_all, preferred_element_type=F32)
        prod[slot, 0] = product[:LANES]
        prod[slot, 1] = product[LANES:]
        core_tail(slot).start()
    for slot in range(slots):
        core_tail(slot).wait_recv()
        pack_out[slot] = prod[slot, c, xl_rows] + prod_in[slot, xl_rows]
        x_tail(slot).start()
    for slot in range(slots):
        x_tail(slot).wait_recv()
        keep = prod[slot, c, my_rows] + prod_in[slot, my_rows]
        cov[:, slot * 2 * LANES : (slot + 1) * 2 * LANES] = (keep + pack_in[slot]) * cov_scale

    def drain(k, carry):
        core_copy(k).wait_send()
        x_copy(k).wait_send()
        return carry

    lax.fori_loop(0, nz, drain, 0)

    def drain_sums(k, carry):
        ring_copy(k).wait_send()
        return carry

    lax.fori_loop(0, nz - 1, drain_sums, 0)
    for copy in blk_sends:
        copy.wait_send()
    forward(0, dev, z, waiting=True)
    for n, (src, origin) in enumerate(forwards):
        forward(n + 1, src, origin, waiting=True)

    def drain_cols(j, carry):
        cols_copy(j).wait_send()
        return carry

    lax.fori_loop(1, nu, drain_cols, 0)
    for i in range(3):
        spec_copy(i).wait_send()
    for slot in range(slots):
        core_tail(slot).wait_send()
        x_tail(slot).wait_send()


def exchange(taken, nz, nu, spec_scale, cov_scale):
    slots = nz // nu
    rows = slots * 2 * LANES
    block = (BLOCK_ROWS, LANES)
    blk = (2 * QUARTER, LANES)
    vmem = pl.BlockSpec(memory_space=pltpu.VMEM)

    def buf(*shape):
        return pltpu.VMEM(shape, F32)

    def dma(*shape):
        return pltpu.SemaphoreType.DMA(shape)

    spectra, cov = pl.pallas_call(
        functools.partial(exchange_kernel, nz, nu, spec_scale, cov_scale),
        out_shape=(
            jax.ShapeDtypeStruct((LANES // 2, 4 * QUARTER), F32),
            jax.ShapeDtypeStruct((LANES // 2, rows), F32),
        ),
        in_specs=[vmem] * len(taken),
        out_specs=(vmem, vmem),
        scratch_shapes=[
            buf(2, nz, 2, *block),
            buf(nz, 2, *block),
            buf(nz, 2, *block),
            buf(nz, *block),
            buf(nz - 1, *block), buf(nz - 1, *block),
            buf(*block), buf(*blk),
            buf(nz - 1, *blk),
            buf(slots, nu, *blk), buf(nu, *blk),
            buf(4, QUARTER, LANES),
            buf(slots, 2, LANES, 2 * LANES), buf(slots, LANES, 2 * LANES),
            buf(slots, LANES // 2, 2 * LANES), buf(slots, LANES // 2, 2 * LANES),
            dma(nz), dma(nz), dma(nz), dma(nz),
            dma(nz - 1), dma(nz - 1),
            dma(nz - 1), dma(nz - 1),
            dma(nz), dma(slots, nu), dma(nu), dma(nu),
            dma(3), dma(3), dma(2, slots), dma(2, slots),
        ],
        compiler_params=pltpu.CompilerParams(
            collective_id=0, has_side_effects=True, vmem_limit_bytes=VMEM_GRANT
        ),
        name="exchange",
    )(*taken)
    return spectra, cov.T


def body(responses, event_bins, nominal_weight, throws):
    nz = lax.axis_size("ev") // 4
    nu = lax.axis_size("uni")
    bins_total = nz * 2 * LANES
    per_bin = event_bins.shape[0] * lax.axis_size("ev") // bins_total
    universes = throws.shape[1] * nu
    rows = event_bins.shape[0] // LANES
    inputs = [
        pltpu.with_memory_space_constraint(x, pltpu.HBM)
        for x in (
            responses, event_bins.reshape(rows, LANES), nominal_weight.reshape(rows, LANES), throws
        )
    ]
    taken = windows(*inputs, nz)
    return exchange(taken, nz, nu, 1.0 / per_bin, 1.0 / (universes * per_bin))


def solution(mesh):
    in_specs = (P(None, "ev"), P("ev"), P("ev"), P(None, "uni"))
    out_specs = (P("ev", "uni"), P("uni", "ev"))
    return jax.shard_map(body, mesh=mesh, in_specs=in_specs, out_specs=out_specs, check_vma=False)
```

```python
import functools

import jax
import jax.numpy as jnp
from jax import lax
from jax.experimental import pallas as pl
from jax.experimental.pallas import tpu as pltpu
from jax.sharding import PartitionSpec as P

LANES = 128
QUARTER = 32
BLOCK_ROWS = 72
CHUNK = 512
WINDOW = 1280
HOP = 3
VMEM_GRANT = 20 << 20
MESH = pl.DeviceIdType.MESH
F32 = jnp.float32


def block_histogram(weights, local):
    iota = lax.broadcasted_iota(jnp.int32, (2 * LANES, local.shape[1]), 0)
    onehot = jnp.where(iota == local, 1.0, 0.0).astype(jnp.bfloat16)
    return lax.dot_general(
        weights, onehot, (((1,), (1,)), ((), ())), preferred_element_type=F32
    )


def weigh(knob_throws, resp, nominal_row):
    log_weight = jnp.dot(knob_throws, resp, preferred_element_type=F32)
    return (nominal_row * jnp.exp(log_weight)).astype(jnp.bfloat16)


def central_rows(nominal_row):
    return jnp.broadcast_to(nominal_row, (16, nominal_row.shape[1])).astype(jnp.bfloat16)


def rows_of(ref, start, count):
    return jnp.concatenate([ref[pl.ds(start + g, 1), :] for g in range(count)], axis=1)


def quarter_blocks(sums):
    row = lax.broadcasted_iota(jnp.int32, (8, LANES), 0)
    tail = sums[4 * QUARTER : 4 * QUARTER + 8]
    central = jnp.where(row == 0, tail[:, :LANES], tail[:, LANES:])
    for quarter in range(4):
        mine = sums[quarter * QUARTER : (quarter + 1) * QUARTER]
        block = jnp.concatenate([mine[:, :LANES], mine[:, LANES:], central], axis=0)
        yield quarter % 2, quarter // 2, block


def windows_kernel(
    resp_hbm, bins_hbm, nominal_hbm, throws_hbm,
    resp_of, local_of, nominal_of, throws_t, extra,
    resp, bins, nominal, throws, nominal_rows, acc, starts, sems, resp_sems,
):
    nz = resp_of.shape[0]
    per_row = LANES
    rows = bins_hbm.shape[0]
    window = WINDOW // LANES
    loads = [
        pltpu.make_async_copy(src, dst, sems.at[i])
        for i, (src, dst) in enumerate(
            [(bins_hbm, bins), (nominal_hbm, nominal), (throws_hbm, throws)]
        )
    ]
    for load in loads:
        load.start()

    def clear(zb, carry):
        extra[:, zb] = jnp.zeros((2, 2, BLOCK_ROWS, LANES), F32)
        return carry

    lax.fori_loop(0, nz, clear, 0)
    for load in loads:
        load.wait()
    all_bins = bins[...]
    below = [jnp.int32(0)]
    for zb in range(1, nz):
        hits = jnp.sum(jnp.where(all_bins < zb * 2 * LANES, 1.0, 0.0), axis=0, keepdims=True)
        below.append(jnp.sum(hits).astype(jnp.int32))
    below.append(jnp.int32(rows * LANES))
    beyond = jnp.int32(0)
    for zb in range(nz):
        start = jnp.minimum(below[zb] // LANES, rows - window)
        starts[zb] = start
        beyond = jnp.maximum(beyond, below[zb + 1] - (start + window) * LANES)

    def resp_copy(zb):
        events = pl.ds(pl.multiple_of(starts[zb] * LANES, LANES), WINDOW)
        return pltpu.make_async_copy(resp_hbm.at[:, events], resp_of.at[zb], resp_sems.at[zb])

    def start_copy(zb, carry):
        resp_copy(zb).start()
        return carry

    lax.fori_loop(0, nz, start_copy, 0)
    nominal_rows[...] = nominal[...].astype(F32)
    knob_throws = throws[...].astype(F32).T.astype(jnp.bfloat16)
    throws_t[...] = knob_throws

    def take(zb, carry):
        at = starts[zb]
        for g in range(window):
            lanes = slice(g * LANES, (g + 1) * LANES)
            local_of[zb, :, lanes] = bins[pl.ds(at + g, 1), :] - zb * 2 * LANES
            nominal_of[zb, :, lanes] = nominal_rows[pl.ds(at + g, 1), :]
        return carry

    lax.fori_loop(0, nz, take, 0)

    @pl.when(beyond > 0)
    def _():
        copy = pltpu.make_async_copy(resp_hbm, resp, sems.at[3])
        copy.start()
        copy.wait()
        count = CHUNK // LANES

        def one_block(zb, carry):
            acc[...] = jnp.zeros(acc.shape, F32)
            first = starts[zb] + window

            def one_chunk(row, c):
                at = jnp.minimum(row, rows - count)
                nominal_row = rows_of(nominal_rows, at, count)
                events = pl.ds(pl.multiple_of(at * LANES, LANES), CHUNK)
                index = at * LANES + lax.broadcasted_iota(jnp.int32, (1, CHUNK), 1)
                bin_row = jnp.where(index >= row * LANES, rows_of(bins, at, count), -1)
                all_weights = jnp.concatenate(
                    [weigh(knob_throws, resp[:, events], nominal_row), central_rows(nominal_row)],
                    axis=0,
                )
                acc[...] += block_histogram(all_weights, bin_row - zb * 2 * LANES)
                return c

            def step(i, c):
                row = first + i * count

                @pl.when(row < rows)
                def _():
                    @pl.when(bins_row_min(bins, row) < (zb + 1) * 2 * LANES)
                    def _():
                        one_chunk(row, 0)

                return c

            lax.fori_loop(0, rows // count, step, 0)
            for c, x, block in quarter_blocks(acc[...]):
                extra[c, zb, x] = block
            return carry

        lax.fori_loop(0, nz, one_block, 0)

    def wait_copy(zb, carry):
        resp_copy(zb).wait()
        return carry

    lax.fori_loop(0, nz, wait_copy, 0)


def bins_row_min(bins, row):
    return jnp.min(bins[pl.ds(row, 1), :])


def windows(responses, bins, nominal, throws, nz):
    rows = bins.shape[0]
    hbm = pl.BlockSpec(memory_space=pltpu.HBM)
    vmem = pl.BlockSpec(memory_space=pltpu.VMEM)
    shape = jax.ShapeDtypeStruct
    return pl.pallas_call(
        windows_kernel,
        out_shape=(
            shape((nz, responses.shape[0], WINDOW), responses.dtype),
            shape((nz, 1, WINDOW), jnp.int32),
            shape((nz, 1, WINDOW), F32),
            shape(throws.shape[::-1], jnp.bfloat16),
            shape((2, nz, 2, BLOCK_ROWS, LANES), F32),
        ),
        in_specs=[hbm] * 4,
        out_specs=(vmem,) * 5,
        scratch_shapes=[
            pltpu.VMEM(responses.shape, responses.dtype),
            pltpu.VMEM(bins.shape, jnp.int32),
            pltpu.VMEM(nominal.shape, nominal.dtype),
            pltpu.VMEM(throws.shape, throws.dtype),
            pltpu.VMEM((rows, LANES), F32),
            pltpu.VMEM((4 * QUARTER + 16, 2 * LANES), F32),
            pltpu.SMEM((nz,), jnp.int32),
            pltpu.SemaphoreType.DMA((4,)),
            pltpu.SemaphoreType.DMA((nz,)),
        ],
        compiler_params=pltpu.CompilerParams(vmem_limit_bytes=VMEM_GRANT),
        name="windows",
    )(responses, bins, nominal, throws)


def exchange_kernel(
    nz, nu, spec_scale, cov_scale,
    resp_of, local_of, nominal_of, throws_t, extra,
    spectra, cov,
    part,
    core_in, summed, x_in, ring_out, ring_in, own, dev, blocks,
    rows_in, cols_in, spec_in, prod, prod_in, pack_out, pack_in,
    core_s, core_r, x_s, x_r, ring_s, ring_r,
    blk_s, blk_r, fwd_s, rows_r, cols_s, cols_r, spec_s, spec_r, tail_s, tail_r,
):
    ev = lax.axis_index("ev")
    u = lax.axis_index("uni")
    z = ev // 4
    xl = lax.rem(ev // 2, 2)
    c = lax.rem(ev, 2)
    core_ev = ev + 1 - 2 * c
    x_ev = ev + 2 - 4 * xl
    diag_ev = x_ev + 1 - 2 * c
    half = nz // 2
    slots = nz // nu
    relays = half // HOP

    def relay_of(d):
        return min((d + 1) // HOP, relays)

    targets = {r: [] for r in range(-relays, relays + 1)}
    for d in range(1 - half, half + 1):
        targets[relay_of(d)].append(d - HOP * relay_of(d))

    def along(d):
        return lax.rem(ev + 4 * (d % nz), 4 * nz)

    def z_at(d):
        return lax.rem(z + d % nz, nz)

    def send(src, dst, ssem, rsem, to_ev=ev, to_u=u):
        return pltpu.make_async_remote_copy(
            src_ref=src, dst_ref=dst, send_sem=ssem, recv_sem=rsem,
            device_id={"ev": to_ev, "uni": to_u}, device_id_type=MESH,
        )

    def block_of(k):
        j = (k + 1) // 2
        away = jnp.where(lax.rem(k, 2) == 1, half - j, nz - half + j)
        return lax.rem(z + away, nz)

    def tell(to_ev, to_u=u):
        pl.semaphore_signal(
            barrier, inc=1, device_id={"ev": to_ev, "uni": to_u}, device_id_type=MESH
        )

    barrier = pltpu.get_barrier_semaphore()
    peers = [core_ev, x_ev, diag_ev]
    for d in sorted({1} | {HOP * r for r in range(1, relays + 1)}):
        peers += [along(d), along(-d)]
    for peer in peers:
        tell(peer)
    for j in range(1, nu):
        tell(ev, lax.rem(u + j, nu))
    expected = len(peers) + nu - 1
    for slot in range(slots):
        d = lax.rem(z - (u * slots + slot) + nz + half - 1, nz) - (half - 1)
        relay = jnp.minimum((d + 1 + HOP * nz) // HOP - nz, relays)
        away = d - HOP * relay
        from_ev = lax.rem(ev + 4 * (nz - away), 4 * nz)

        def tell_column(v, carry, from_ev=from_ev):
            @pl.when((from_ev != ev) | (v != u))
            def _():
                tell(from_ev, v)

            return carry

        lax.fori_loop(0, nu, tell_column, 0)
    for r, aways in targets.items():
        for away in aways:
            if away == 0:
                expected = expected + jnp.where(z_at(-HOP * r) // slots == u, 0, 1)
            else:
                expected = expected + 1
    knob_throws = throws_t[...]
    pl.semaphore_wait(barrier, expected)

    def core_copy(k):
        zb = block_of(k)
        return send(part.at[1 - c, zb], core_in.at[zb], core_s.at[k], core_r.at[k], to_ev=core_ev)

    def x_copy(k):
        zb = block_of(k)
        return send(summed.at[zb, 1 - xl], x_in.at[zb], x_s.at[k], x_r.at[k], to_ev=x_ev)

    def histogram(k):
        zb = block_of(k)
        nominal_row = nominal_of[zb]
        weights = jnp.concatenate(
            [weigh(knob_throws, resp_of[zb], nominal_row), central_rows(nominal_row)], axis=0
        )
        sums = block_histogram(weights, local_of[zb])
        for to_core, to_x, block in quarter_blocks(sums):
            part[to_core, zb, to_x] = block + extra[to_core, zb, to_x]
        core_copy(k).start()

    def start_x(k):
        zb = block_of(k)
        core_copy(k).wait_recv()
        summed[zb] = part[c, zb] + core_in[zb]
        x_copy(k).start()

    def ring_copy(k):
        d, way = half - (k + 1) // 2, 1 if k % 2 or k == 0 else -1
        to = d if d == 1 or d % HOP == 0 else 1
        return send(
            ring_out.at[k], ring_in.at[k], ring_s.at[k], ring_r.at[k], to_ev=along(way * to)
        )

    def starts_chain(k):
        return k in (0, 2) or (half - (k + 1) // 2) % HOP == HOP - 1

    def sum_step(k):
        zb = block_of(k)
        x_copy(k).wait_recv()
        value = summed[zb, xl] + x_in[zb]
        if not starts_chain(k):
            before = max(k - 2, 0)
            ring_copy(before).wait_recv()
            value = value + ring_in[before]
        ring_out[k] = value
        ring_copy(k).start()

    def block_step(k, carry):
        histogram(k)

        @pl.when(k > 0)
        def _():
            start_x(k - 1)

        return carry

    when = {}
    for k in range(nz - 1):
        when[k] = 4.2 + 0.79 * k
        if not starts_chain(k):
            when[k] = max(when[k], when[max(k - 2, 0)] + 3.1)
    done = 0
    for k in sorted(when, key=when.get):
        count = min(nz, max(int(when[k] / 0.65), k + 2, done))
        if count > done:
            lax.fori_loop(done, count, block_step, 0)
        if count == nz and done < nz:
            start_x(nz - 1)
        done = count
        sum_step(k)
    x_copy(nz - 1).wait_recv()
    total = summed[z, xl] + x_in[z]
    for k in range(nz - 1):
        d = half - (k + 1) // 2
        if d == 1 or d % HOP == 0:
            ring_copy(k).wait_recv()
            total = total + ring_in[k]
    own[...] = total
    dev[:QUARTER] = total[:QUARTER] - total[2 * QUARTER : 2 * QUARTER + 1]
    dev[QUARTER:] = total[QUARTER : 2 * QUARTER] - total[2 * QUARTER + 1 : 2 * QUARTER + 2]

    def relay_copy(r, src):
        n = 2 * (abs(r) - 1) + (r < 0)
        return send(
            src, blocks.at[n], blk_s.at[n], blk_r.at[n], to_ev=along(HOP if r > 0 else -HOP)
        )

    def direct(r, src, waiting=False):
        origin = z_at(-HOP * r)
        owner = origin // slots
        slot = lax.rem(origin, slots)
        for away in targets[r]:
            n = HOP * r + away + half - 1
            copy = send(
                src, rows_in.at[slot, u], fwd_s.at[n], rows_r.at[slot, u],
                to_ev=along(away), to_u=owner,
            )
            run = copy.wait_send if waiting else copy.start
            if away:
                run()
                continue
            pl.when(owner != u)(run)
            if not waiting:

                @pl.when(owner == u)
                def _():
                    rows_in[slot, u] = src[...]

    if relays:
        relay_copy(1, dev).start()
        relay_copy(-1, dev).start()

    def cols_copy(j):
        return send(dev, cols_in.at[u], cols_s.at[j], cols_r.at[u], to_u=lax.rem(u + j, nu))

    def start_cols(j, carry):
        cols_copy(j).start()
        return carry

    direct(0, dev)
    lax.fori_loop(1, nu, start_cols, 0)
    cols_in[u] = dev[...]

    mine = 2 * xl + c
    spec_peers = ((core_ev, xl), (x_ev, 1 - xl), (diag_ev, 1 - xl))

    def spec_copy(i):
        peer, peer_half = spec_peers[i]
        src = own.at[pl.ds(pl.multiple_of(peer_half * QUARTER, QUARTER), QUARTER)]
        return send(src, spec_in.at[mine], spec_s.at[i], spec_r.at[i], to_ev=peer)

    for i in range(3):
        spec_copy(i).start()
    spec_in[mine] = own[pl.ds(pl.multiple_of(xl * QUARTER, QUARTER), QUARTER)]

    def block_of_relay(r):
        return blocks.at[2 * (abs(r) - 1) + (r < 0)]

    for r in range(1, relays + 1):
        for relay in (r, -r):
            relay_copy(relay, dev).wait_recv()
            if r < relays:
                relay_copy(relay + (1 if relay > 0 else -1), block_of_relay(relay)).start()
        for relay in (r, -r):
            direct(relay, block_of_relay(relay))

    for i in range(3):
        spec_copy(i).wait_recv()
    by_bin = spec_in[...].reshape(4 * QUARTER, LANES).T
    spectra[...] = jnp.where(c == 0, by_bin[: LANES // 2], by_bin[LANES // 2 :]) * spec_scale

    def wait_cols(j, carry):
        v = lax.rem(u + j, nu)
        send(dev, cols_in.at[v], cols_s.at[j], cols_r.at[v], to_u=v).wait_recv()
        return carry

    lax.fori_loop(1, nu, wait_cols, 0)

    depth = nu * QUARTER
    bf16 = jnp.bfloat16
    lane = lax.broadcasted_iota(jnp.int32, (depth, LANES), 1)
    left = cols_in[:, :QUARTER].reshape(depth, LANES)
    right = cols_in[:, QUARTER:].reshape(depth, LANES)
    cols = jnp.concatenate(
        [
            jnp.where(lane < LANES // 2, left, pltpu.roll(right, LANES // 2, 1)).T,
            jnp.where(lane < LANES // 2, pltpu.roll(left, LANES // 2, 1), right).T,
        ],
        axis=0,
    )
    cols_hi = cols.astype(bf16)
    cols_lo = (cols - cols_hi.astype(F32)).astype(bf16)
    cols_all = jnp.concatenate([cols_hi, cols_hi, cols_lo], axis=1)
    xl_rows = pl.ds(pl.multiple_of((1 - xl) * (LANES // 2), LANES // 2), LANES // 2)
    my_rows = pl.ds(pl.multiple_of(xl * (LANES // 2), LANES // 2), LANES // 2)

    def core_tail(slot):
        return send(
            prod.at[slot, 1 - c], prod_in.at[slot], tail_s.at[0, slot], tail_r.at[0, slot],
            to_ev=core_ev,
        )

    def x_tail(slot):
        return send(
            pack_out.at[slot], pack_in.at[slot], tail_s.at[1, slot], tail_r.at[1, slot], to_ev=x_ev
        )

    def local_rows(slot):
        d = lax.rem(z - (u * slots + slot) + nz + half - 1, nz) - (half - 1)
        relay = jnp.minimum((d + 1 + HOP * nz) // HOP - nz, relays)
        return d == HOP * relay

    from_below = lax.rem(z - u * slots + nz, nz) <= half
    for i in range(slots):
        slot = jnp.where(from_below, slots - 1 - i, i)

        def wait_rows(j, carry, slot=slot):
            v = lax.rem(u + j, nu)
            send(dev, rows_in.at[slot, v], cols_s.at[0], rows_r.at[slot, v], to_ev=core_ev).wait_recv()
            return carry

        @pl.when(jnp.logical_not(local_rows(slot)))
        def _(wait_rows=wait_rows):
            wait_rows(0, 0)

        lax.fori_loop(1, nu, wait_rows, 0)
        rows = jnp.concatenate(
            [
                rows_in[slot, :, :QUARTER].reshape(depth, LANES),
                rows_in[slot, :, QUARTER:].reshape(depth, LANES),
            ],
            axis=1,
        )
        rows_hi = rows.astype(bf16)
        rows_lo = (rows - rows_hi.astype(F32)).astype(bf16)
        rows_all = jnp.concatenate([rows_hi, rows_lo, rows_hi], axis=0)
        product = jnp.dot(cols_all, rows_all, preferred_element_type=F32)
        prod[slot, 0] = product[:LANES]
        prod[slot, 1] = product[LANES:]
        core_tail(slot).start()
    for i in range(slots):
        slot = jnp.where(from_below, slots - 1 - i, i)
        core_tail(slot).wait_recv()
        pack_out[slot] = prod[slot, c, xl_rows] + prod_in[slot, xl_rows]
        x_tail(slot).start()
    for slot in range(slots):
        x_tail(slot).wait_recv()
        keep = prod[slot, c, my_rows] + prod_in[slot, my_rows]
        cov[:, slot * 2 * LANES : (slot + 1) * 2 * LANES] = (keep + pack_in[slot]) * cov_scale

    def drain(k, carry):
        core_copy(k).wait_send()
        x_copy(k).wait_send()
        return carry

    lax.fori_loop(0, nz, drain, 0)

    for k in range(nz - 1):
        ring_copy(k).wait_send()
    for r in range(-relays, relays + 1):
        if r:
            relay_copy(r, dev).wait_send()
        direct(r, dev, waiting=True)

    def drain_cols(j, carry):
        cols_copy(j).wait_send()
        return carry

    lax.fori_loop(1, nu, drain_cols, 0)
    for i in range(3):
        spec_copy(i).wait_send()
    for slot in range(slots):
        core_tail(slot).wait_send()
        x_tail(slot).wait_send()


def exchange(taken, nz, nu, spec_scale, cov_scale):
    slots = nz // nu
    rows = slots * 2 * LANES
    block = (BLOCK_ROWS, LANES)
    blk = (2 * QUARTER, LANES)
    vmem = pl.BlockSpec(memory_space=pltpu.VMEM)

    def buf(*shape):
        return pltpu.VMEM(shape, F32)

    def dma(*shape):
        return pltpu.SemaphoreType.DMA(shape)

    spectra, cov = pl.pallas_call(
        functools.partial(exchange_kernel, nz, nu, spec_scale, cov_scale),
        out_shape=(
            jax.ShapeDtypeStruct((LANES // 2, 4 * QUARTER), F32),
            jax.ShapeDtypeStruct((LANES // 2, rows), F32),
        ),
        in_specs=[vmem] * len(taken),
        out_specs=(vmem, vmem),
        scratch_shapes=[
            buf(2, nz, 2, *block),
            buf(nz, 2, *block),
            buf(nz, 2, *block),
            buf(nz, *block),
            buf(nz - 1, *block), buf(nz - 1, *block),
            buf(*block), buf(*blk),
            buf(2 * max(1, nz // 2 // HOP), *blk),
            buf(slots, nu, *blk), buf(nu, *blk),
            buf(4, QUARTER, LANES),
            buf(slots, 2, LANES, 2 * LANES), buf(slots, LANES, 2 * LANES),
            buf(slots, LANES // 2, 2 * LANES), buf(slots, LANES // 2, 2 * LANES),
            dma(nz), dma(nz), dma(nz), dma(nz),
            dma(nz - 1), dma(nz - 1),
            dma(2 * max(1, nz // 2 // HOP)), dma(2 * max(1, nz // 2 // HOP)),
            dma(nz), dma(slots, nu), dma(nu), dma(nu),
            dma(3), dma(3), dma(2, slots), dma(2, slots),
        ],
        compiler_params=pltpu.CompilerParams(
            collective_id=0, has_side_effects=True, vmem_limit_bytes=VMEM_GRANT
        ),
        name="exchange",
    )(*taken)
    return spectra, cov.T


def body(responses, event_bins, nominal_weight, throws):
    nz = lax.axis_size("ev") // 4
    nu = lax.axis_size("uni")
    bins_total = nz * 2 * LANES
    per_bin = event_bins.shape[0] * lax.axis_size("ev") // bins_total
    universes = throws.shape[1] * nu
    rows = event_bins.shape[0] // LANES
    inputs = [
        pltpu.with_memory_space_constraint(x, pltpu.HBM)
        for x in (
            responses, event_bins.reshape(rows, LANES), nominal_weight.reshape(rows, LANES), throws
        )
    ]
    taken = windows(*inputs, nz)
    return exchange(taken, nz, nu, 1.0 / per_bin, 1.0 / (universes * per_bin))


def solution(mesh):
    in_specs = (P(None, "ev"), P("ev"), P("ev"), P(None, "uni"))
    out_specs = (P("ev", "uni"), P("uni", "ev"))
    return jax.shard_map(body, mesh=mesh, in_specs=in_specs, out_specs=out_specs, check_vma=False)
```

```python
import functools

import jax
import jax.numpy as jnp
from jax import lax
from jax.experimental import pallas as pl
from jax.experimental.pallas import tpu as pltpu
from jax.sharding import PartitionSpec as P

LANES = 128
QUARTER = 32
BLOCK_ROWS = 66
CHUNK = 512
WINDOW = 1280
HOP = 3
VMEM_GRANT = 20 << 20
MESH = pl.DeviceIdType.MESH
F32 = jnp.float32


def block_histogram(weights, local):
    iota = lax.broadcasted_iota(jnp.int32, (2 * LANES, local.shape[1]), 0)
    onehot = jnp.where(iota == local, 1.0, 0.0).astype(jnp.bfloat16)
    return lax.dot_general(
        weights, onehot, (((1,), (1,)), ((), ())), preferred_element_type=F32
    )


def weigh(knob_throws, resp, nominal_row):
    log_weight = jnp.dot(knob_throws, resp, preferred_element_type=F32)
    return (nominal_row * jnp.exp(log_weight)).astype(jnp.bfloat16)


def central_rows(nominal_row):
    return jnp.broadcast_to(nominal_row, (16, nominal_row.shape[1])).astype(jnp.bfloat16)


def rows_of(ref, start, count):
    return jnp.concatenate([ref[pl.ds(start + g, 1), :] for g in range(count)], axis=1)


def quarter_blocks(sums):
    row = lax.broadcasted_iota(jnp.int32, (8, LANES), 0)
    tail = sums[4 * QUARTER : 4 * QUARTER + 8]
    central = jnp.where(row == 0, tail[:, :LANES], tail[:, LANES:])[:2]
    for quarter in range(4):
        mine = sums[quarter * QUARTER : (quarter + 1) * QUARTER]
        block = jnp.concatenate([mine[:, :LANES], mine[:, LANES:], central], axis=0)
        yield quarter % 2, quarter // 2, block


def windows_kernel(
    resp_hbm, bins_hbm, nominal_hbm, throws_hbm,
    resp_of, local_of, nominal_of, throws_t, extra,
    resp, bins, nominal, throws, nominal_rows, acc, starts, sems, resp_sems,
):
    nz = resp_of.shape[0]
    per_row = LANES
    rows = bins_hbm.shape[0]
    window = WINDOW // LANES
    loads = [
        pltpu.make_async_copy(src, dst, sems.at[i])
        for i, (src, dst) in enumerate(
            [(bins_hbm, bins), (nominal_hbm, nominal), (throws_hbm, throws)]
        )
    ]
    for load in loads:
        load.start()

    def clear(zb, carry):
        extra[:, zb] = jnp.zeros((2, 2, BLOCK_ROWS, LANES), F32)
        return carry

    lax.fori_loop(0, nz, clear, 0)
    for load in loads:
        load.wait()
    all_bins = bins[...]
    below = [jnp.int32(0)]
    for zb in range(1, nz):
        hits = jnp.sum(jnp.where(all_bins < zb * 2 * LANES, 1.0, 0.0), axis=0, keepdims=True)
        below.append(jnp.sum(hits).astype(jnp.int32))
    below.append(jnp.int32(rows * LANES))
    beyond = jnp.int32(0)
    for zb in range(nz):
        start = jnp.minimum(below[zb] // LANES, rows - window)
        starts[zb] = start
        beyond = jnp.maximum(beyond, below[zb + 1] - (start + window) * LANES)

    def resp_copy(zb):
        events = pl.ds(pl.multiple_of(starts[zb] * LANES, LANES), WINDOW)
        return pltpu.make_async_copy(resp_hbm.at[:, events], resp_of.at[zb], resp_sems.at[zb])

    def start_copy(zb, carry):
        resp_copy(zb).start()
        return carry

    lax.fori_loop(0, nz, start_copy, 0)
    nominal_rows[...] = nominal[...].astype(F32)
    knob_throws = throws[...].astype(F32).T.astype(jnp.bfloat16)
    throws_t[...] = knob_throws

    def take(zb, carry):
        at = starts[zb]
        for g in range(window):
            lanes = slice(g * LANES, (g + 1) * LANES)
            local_of[zb, :, lanes] = bins[pl.ds(at + g, 1), :] - zb * 2 * LANES
            nominal_of[zb, :, lanes] = nominal_rows[pl.ds(at + g, 1), :]
        return carry

    lax.fori_loop(0, nz, take, 0)

    @pl.when(beyond > 0)
    def _():
        copy = pltpu.make_async_copy(resp_hbm, resp, sems.at[3])
        copy.start()
        copy.wait()
        count = CHUNK // LANES

        def one_block(zb, carry):
            acc[...] = jnp.zeros(acc.shape, F32)
            first = starts[zb] + window

            def one_chunk(row, c):
                at = jnp.minimum(row, rows - count)
                nominal_row = rows_of(nominal_rows, at, count)
                events = pl.ds(pl.multiple_of(at * LANES, LANES), CHUNK)
                index = at * LANES + lax.broadcasted_iota(jnp.int32, (1, CHUNK), 1)
                bin_row = jnp.where(index >= row * LANES, rows_of(bins, at, count), -1)
                all_weights = jnp.concatenate(
                    [weigh(knob_throws, resp[:, events], nominal_row), central_rows(nominal_row)],
                    axis=0,
                )
                acc[...] += block_histogram(all_weights, bin_row - zb * 2 * LANES)
                return c

            def step(i, c):
                row = first + i * count

                @pl.when(row < rows)
                def _():
                    @pl.when(bins_row_min(bins, row) < (zb + 1) * 2 * LANES)
                    def _():
                        one_chunk(row, 0)

                return c

            lax.fori_loop(0, rows // count, step, 0)
            for c, x, block in quarter_blocks(acc[...]):
                extra[c, zb, x] = block
            return carry

        lax.fori_loop(0, nz, one_block, 0)

    def wait_copy(zb, carry):
        resp_copy(zb).wait()
        return carry

    lax.fori_loop(0, nz, wait_copy, 0)


def bins_row_min(bins, row):
    return jnp.min(bins[pl.ds(row, 1), :])


def windows(responses, bins, nominal, throws, nz):
    rows = bins.shape[0]
    hbm = pl.BlockSpec(memory_space=pltpu.HBM)
    vmem = pl.BlockSpec(memory_space=pltpu.VMEM)
    shape = jax.ShapeDtypeStruct
    return pl.pallas_call(
        windows_kernel,
        out_shape=(
            shape((nz, responses.shape[0], WINDOW), responses.dtype),
            shape((nz, 1, WINDOW), jnp.int32),
            shape((nz, 1, WINDOW), F32),
            shape(throws.shape[::-1], jnp.bfloat16),
            shape((2, nz, 2, BLOCK_ROWS, LANES), F32),
        ),
        in_specs=[hbm] * 4,
        out_specs=(vmem,) * 5,
        scratch_shapes=[
            pltpu.VMEM(responses.shape, responses.dtype),
            pltpu.VMEM(bins.shape, jnp.int32),
            pltpu.VMEM(nominal.shape, nominal.dtype),
            pltpu.VMEM(throws.shape, throws.dtype),
            pltpu.VMEM((rows, LANES), F32),
            pltpu.VMEM((4 * QUARTER + 16, 2 * LANES), F32),
            pltpu.SMEM((nz,), jnp.int32),
            pltpu.SemaphoreType.DMA((4,)),
            pltpu.SemaphoreType.DMA((nz,)),
        ],
        compiler_params=pltpu.CompilerParams(vmem_limit_bytes=VMEM_GRANT),
        name="windows",
    )(responses, bins, nominal, throws)


def exchange_kernel(
    nz, nu, spec_scale, cov_scale,
    resp_of, local_of, nominal_of, throws_t, extra,
    spectra, cov,
    part,
    core_in, summed, x_in, ring_out, ring_in, own, dev, blocks,
    rows_in, cols_in, spec_in, prod, prod_in, pack_out, pack_in,
    core_s, core_r, x_s, x_r, ring_s, ring_r,
    blk_s, blk_r, fwd_s, rows_r, cols_s, cols_r, spec_s, spec_r, tail_s, tail_r,
):
    ev = lax.axis_index("ev")
    u = lax.axis_index("uni")
    z = ev // 4
    xl = lax.rem(ev // 2, 2)
    c = lax.rem(ev, 2)
    core_ev = ev + 1 - 2 * c
    x_ev = ev + 2 - 4 * xl
    diag_ev = x_ev + 1 - 2 * c
    half = nz // 2
    slots = nz // nu
    relays = half // HOP

    def relay_of(d):
        return min((d + 1) // HOP, relays)

    targets = {r: [] for r in range(-relays, relays + 1)}
    for d in range(1 - half, half + 1):
        targets[relay_of(d)].append(d - HOP * relay_of(d))

    def along(d):
        return lax.rem(ev + 4 * (d % nz), 4 * nz)

    def z_at(d):
        return lax.rem(z + d % nz, nz)

    def send(src, dst, ssem, rsem, to_ev=ev, to_u=u):
        return pltpu.make_async_remote_copy(
            src_ref=src, dst_ref=dst, send_sem=ssem, recv_sem=rsem,
            device_id={"ev": to_ev, "uni": to_u}, device_id_type=MESH,
        )

    def still_to_go(d):
        end = max(d // HOP * HOP, 1)
        return 3.1 * (d - end) + 2.3 + 0.7 * end

    order = sorted(range(1, half + 1), key=lambda d: -still_to_go(d))
    away_of = [way * d for d in order for way in (1, -1) if way * d > -half] + [0]
    place = {d: k for k, d in enumerate(away_of)}

    def block_of(k):
        if isinstance(k, int):
            return z_at(away_of[k])
        away = sum(jnp.where(k == i, d % nz, 0) for i, d in enumerate(away_of))
        return lax.rem(z + away, nz)

    def tell(to_ev, to_u=u):
        pl.semaphore_signal(
            barrier, inc=1, device_id={"ev": to_ev, "uni": to_u}, device_id_type=MESH
        )

    barrier = pltpu.get_barrier_semaphore()
    peers = [core_ev, x_ev, diag_ev]
    for d in sorted({1} | {HOP * r for r in range(1, relays + 1)}):
        peers += [along(d), along(-d)]
    for peer in peers:
        tell(peer)
    for j in range(1, nu):
        tell(ev, lax.rem(u + j, nu))
    expected = len(peers) + nu - 1
    for slot in range(slots):
        d = lax.rem(z - (u * slots + slot) + nz + half - 1, nz) - (half - 1)
        relay = jnp.minimum((d + 1 + HOP * nz) // HOP - nz, relays)
        away = d - HOP * relay
        from_ev = lax.rem(ev + 4 * (nz - away), 4 * nz)

        def tell_column(v, carry, from_ev=from_ev):
            @pl.when((from_ev != ev) | (v != u))
            def _():
                tell(from_ev, v)

            return carry

        lax.fori_loop(0, nu, tell_column, 0)
    for r, aways in targets.items():
        for away in aways:
            if away == 0:
                expected = expected + jnp.where(z_at(-HOP * r) // slots == u, 0, 1)
            else:
                expected = expected + 1
    knob_throws = throws_t[...]
    pl.semaphore_wait(barrier, expected)

    def core_copy(k):
        zb = block_of(k)
        return send(part.at[1 - c, zb], core_in.at[zb], core_s.at[k], core_r.at[k], to_ev=core_ev)

    def x_copy(k):
        zb = block_of(k)
        return send(summed.at[zb, 1 - xl], x_in.at[zb], x_s.at[k], x_r.at[k], to_ev=x_ev)

    def histogram(k):
        zb = block_of(k)
        nominal_row = nominal_of[zb]
        weights = jnp.concatenate(
            [weigh(knob_throws, resp_of[zb], nominal_row), central_rows(nominal_row)], axis=0
        )
        sums = block_histogram(weights, local_of[zb])
        for to_core, to_x, block in quarter_blocks(sums):
            part[to_core, zb, to_x] = block + extra[to_core, zb, to_x]
        core_copy(k).start()

    def start_x(k):
        zb = block_of(k)
        core_copy(k).wait_recv()
        summed[zb] = part[c, zb] + core_in[zb]
        x_copy(k).start()

    def ring_copy(k):
        d = away_of[k]
        to = d if abs(d) == 1 or d % HOP == 0 else (1 if d > 0 else -1)
        return send(ring_out.at[k], ring_in.at[k], ring_s.at[k], ring_r.at[k], to_ev=along(to))

    def before(k):
        d = away_of[k]
        farther = d + (1 if d > 0 else -1)
        return place.get(farther) if farther % HOP else None

    def sum_step(k):
        zb = block_of(k)
        x_copy(k).wait_recv()
        value = summed[zb, xl] + x_in[zb]
        if before(k) is not None:
            ring_copy(before(k)).wait_recv()
            value = value + ring_in[before(k)]
        ring_out[k] = value
        ring_copy(k).start()

    def block_step(k, carry):
        histogram(k)

        @pl.when(k > 0)
        def _():
            start_x(k - 1)

        return carry

    when = {}
    for k in sorted(range(nz - 1), key=lambda k: -abs(away_of[k])):
        when[k] = max(4.2 + 0.75 * k, when.get(before(k), 0.0) + 3.1)
    done = 0
    for k in sorted(when, key=when.get):
        count = min(nz, max(int(when[k] / 0.65), k + 2, done))
        if count > done:
            lax.fori_loop(done, count, block_step, 0)
        if count == nz and done < nz:
            start_x(nz - 1)
        done = count
        sum_step(k)
    x_copy(nz - 1).wait_recv()
    total = summed[z, xl] + x_in[z]
    for k in range(nz - 1):
        if abs(away_of[k]) == 1 or away_of[k] % HOP == 0:
            ring_copy(k).wait_recv()
            total = total + ring_in[k]
    own[...] = total
    dev[:QUARTER] = total[:QUARTER] - total[2 * QUARTER : 2 * QUARTER + 1]
    dev[QUARTER:] = total[QUARTER : 2 * QUARTER] - total[2 * QUARTER + 1 : 2 * QUARTER + 2]

    def relay_copy(r, src):
        n = 2 * (abs(r) - 1) + (r < 0)
        return send(
            src, blocks.at[n], blk_s.at[n], blk_r.at[n], to_ev=along(HOP if r > 0 else -HOP)
        )

    def direct(r, src, waiting=False):
        origin = z_at(-HOP * r)
        owner = origin // slots
        slot = lax.rem(origin, slots)
        for away in targets[r]:
            n = HOP * r + away + half - 1
            copy = send(
                src, rows_in.at[slot, u], fwd_s.at[n], rows_r.at[slot, u],
                to_ev=along(away), to_u=owner,
            )
            run = copy.wait_send if waiting else copy.start
            if away:
                run()
                continue
            pl.when(owner != u)(run)
            if not waiting:

                @pl.when(owner == u)
                def _():
                    rows_in[slot, u] = src[...]

    if relays:
        relay_copy(1, dev).start()
        relay_copy(-1, dev).start()

    def cols_copy(j):
        return send(dev, cols_in.at[u], cols_s.at[j], cols_r.at[u], to_u=lax.rem(u + j, nu))

    def start_cols(j, carry):
        cols_copy(j).start()
        return carry

    direct(0, dev)
    lax.fori_loop(1, nu, start_cols, 0)
    cols_in[u] = dev[...]

    mine = 2 * xl + c
    spec_peers = ((core_ev, xl), (x_ev, 1 - xl), (diag_ev, 1 - xl))

    def spec_copy(i):
        peer, peer_half = spec_peers[i]
        src = own.at[pl.ds(pl.multiple_of(peer_half * QUARTER, QUARTER), QUARTER)]
        return send(src, spec_in.at[mine], spec_s.at[i], spec_r.at[i], to_ev=peer)

    for i in range(3):
        spec_copy(i).start()
    spec_in[mine] = own[pl.ds(pl.multiple_of(xl * QUARTER, QUARTER), QUARTER)]

    def block_of_relay(r):
        return blocks.at[2 * (abs(r) - 1) + (r < 0)]

    for r in range(1, relays + 1):
        for relay in (r, -r):
            relay_copy(relay, dev).wait_recv()
            if r < relays:
                relay_copy(relay + (1 if relay > 0 else -1), block_of_relay(relay)).start()
        for relay in (r, -r):
            direct(relay, block_of_relay(relay))

    for i in range(3):
        spec_copy(i).wait_recv()
    by_bin = spec_in[...].reshape(4 * QUARTER, LANES).T
    spectra[...] = jnp.where(c == 0, by_bin[: LANES // 2], by_bin[LANES // 2 :]) * spec_scale

    def wait_cols(j, carry):
        v = lax.rem(u + j, nu)
        send(dev, cols_in.at[v], cols_s.at[j], cols_r.at[v], to_u=v).wait_recv()
        return carry

    lax.fori_loop(1, nu, wait_cols, 0)

    depth = nu * QUARTER
    bf16 = jnp.bfloat16
    lane = lax.broadcasted_iota(jnp.int32, (depth, LANES), 1)
    left = cols_in[:, :QUARTER].reshape(depth, LANES)
    right = cols_in[:, QUARTER:].reshape(depth, LANES)
    cols = jnp.concatenate(
        [
            jnp.where(lane < LANES // 2, left, pltpu.roll(right, LANES // 2, 1)).T,
            jnp.where(lane < LANES // 2, pltpu.roll(left, LANES // 2, 1), right).T,
        ],
        axis=0,
    )
    cols_hi = cols.astype(bf16)
    cols_lo = (cols - cols_hi.astype(F32)).astype(bf16)
    cols_all = jnp.concatenate([cols_hi, cols_hi, cols_lo], axis=1)
    xl_rows = pl.ds(pl.multiple_of((1 - xl) * (LANES // 2), LANES // 2), LANES // 2)
    my_rows = pl.ds(pl.multiple_of(xl * (LANES // 2), LANES // 2), LANES // 2)

    def core_tail(slot):
        return send(
            prod.at[slot, 1 - c], prod_in.at[slot], tail_s.at[0, slot], tail_r.at[0, slot],
            to_ev=core_ev,
        )

    def x_tail(slot):
        return send(
            pack_out.at[slot], pack_in.at[slot], tail_s.at[1, slot], tail_r.at[1, slot], to_ev=x_ev
        )

    def local_rows(slot):
        d = lax.rem(z - (u * slots + slot) + nz + half - 1, nz) - (half - 1)
        relay = jnp.minimum((d + 1 + HOP * nz) // HOP - nz, relays)
        return d == HOP * relay

    from_below = lax.rem(z - u * slots + nz, nz) <= half
    for i in range(slots):
        slot = jnp.where(from_below, slots - 1 - i, i)

        def wait_rows(j, carry, slot=slot):
            v = lax.rem(u + j, nu)
            send(dev, rows_in.at[slot, v], cols_s.at[0], rows_r.at[slot, v], to_ev=core_ev).wait_recv()
            return carry

        @pl.when(jnp.logical_not(local_rows(slot)))
        def _(wait_rows=wait_rows):
            wait_rows(0, 0)

        lax.fori_loop(1, nu, wait_rows, 0)
        rows = jnp.concatenate(
            [
                rows_in[slot, :, :QUARTER].reshape(depth, LANES),
                rows_in[slot, :, QUARTER:].reshape(depth, LANES),
            ],
            axis=1,
        )
        rows_hi = rows.astype(bf16)
        rows_lo = (rows - rows_hi.astype(F32)).astype(bf16)
        rows_all = jnp.concatenate([rows_hi, rows_lo, rows_hi], axis=0)
        product = jnp.dot(cols_all, rows_all, preferred_element_type=F32)
        prod[slot, 0] = product[:LANES]
        prod[slot, 1] = product[LANES:]
        core_tail(slot).start()
    for i in range(slots):
        slot = jnp.where(from_below, slots - 1 - i, i)
        core_tail(slot).wait_recv()
        pack_out[slot] = prod[slot, c, xl_rows] + prod_in[slot, xl_rows]
        x_tail(slot).start()
    for slot in range(slots):
        x_tail(slot).wait_recv()
        keep = prod[slot, c, my_rows] + prod_in[slot, my_rows]
        cov[:, slot * 2 * LANES : (slot + 1) * 2 * LANES] = (keep + pack_in[slot]) * cov_scale

    def drain(k, carry):
        core_copy(k).wait_send()
        x_copy(k).wait_send()
        return carry

    lax.fori_loop(0, nz, drain, 0)

    for k in range(nz - 1):
        ring_copy(k).wait_send()
    for r in range(-relays, relays + 1):
        if r:
            relay_copy(r, dev).wait_send()
        direct(r, dev, waiting=True)

    def drain_cols(j, carry):
        cols_copy(j).wait_send()
        return carry

    lax.fori_loop(1, nu, drain_cols, 0)
    for i in range(3):
        spec_copy(i).wait_send()
    for slot in range(slots):
        core_tail(slot).wait_send()
        x_tail(slot).wait_send()


def exchange(taken, nz, nu, spec_scale, cov_scale):
    slots = nz // nu
    rows = slots * 2 * LANES
    block = (BLOCK_ROWS, LANES)
    blk = (2 * QUARTER, LANES)
    vmem = pl.BlockSpec(memory_space=pltpu.VMEM)

    def buf(*shape):
        return pltpu.VMEM(shape, F32)

    def dma(*shape):
        return pltpu.SemaphoreType.DMA(shape)

    spectra, cov = pl.pallas_call(
        functools.partial(exchange_kernel, nz, nu, spec_scale, cov_scale),
        out_shape=(
            jax.ShapeDtypeStruct((LANES // 2, 4 * QUARTER), F32),
            jax.ShapeDtypeStruct((LANES // 2, rows), F32),
        ),
        in_specs=[vmem] * len(taken),
        out_specs=(vmem, vmem),
        scratch_shapes=[
            buf(2, nz, 2, *block),
            buf(nz, 2, *block),
            buf(nz, 2, *block),
            buf(nz, *block),
            buf(nz - 1, *block), buf(nz - 1, *block),
            buf(*block), buf(*blk),
            buf(2 * max(1, nz // 2 // HOP), *blk),
            buf(slots, nu, *blk), buf(nu, *blk),
            buf(4, QUARTER, LANES),
            buf(slots, 2, LANES, 2 * LANES), buf(slots, LANES, 2 * LANES),
            buf(slots, LANES // 2, 2 * LANES), buf(slots, LANES // 2, 2 * LANES),
            dma(nz), dma(nz), dma(nz), dma(nz),
            dma(nz - 1), dma(nz - 1),
            dma(2 * max(1, nz // 2 // HOP)), dma(2 * max(1, nz // 2 // HOP)),
            dma(nz), dma(slots, nu), dma(nu), dma(nu),
            dma(3), dma(3), dma(2, slots), dma(2, slots),
        ],
        compiler_params=pltpu.CompilerParams(
            collective_id=0, has_side_effects=True, vmem_limit_bytes=VMEM_GRANT
        ),
        name="exchange",
    )(*taken)
    return spectra, cov.T


def body(responses, event_bins, nominal_weight, throws):
    nz = lax.axis_size("ev") // 4
    nu = lax.axis_size("uni")
    bins_total = nz * 2 * LANES
    per_bin = event_bins.shape[0] * lax.axis_size("ev") // bins_total
    universes = throws.shape[1] * nu
    rows = event_bins.shape[0] // LANES
    inputs = [
        pltpu.with_memory_space_constraint(x, pltpu.HBM)
        for x in (
            responses, event_bins.reshape(rows, LANES), nominal_weight.reshape(rows, LANES), throws
        )
    ]
    taken = windows(*inputs, nz)
    return exchange(taken, nz, nu, 1.0 / per_bin, 1.0 / (universes * per_bin))


def solution(mesh):
    in_specs = (P(None, "ev"), P("ev"), P("ev"), P(None, "uni"))
    out_specs = (P("ev", "uni"), P("uni", "ev"))
    return jax.shard_map(body, mesh=mesh, in_specs=in_specs, out_specs=out_specs, check_vma=False)
```

```python
import functools

import jax
import jax.numpy as jnp
from jax import lax
from jax.experimental import pallas as pl
from jax.experimental.pallas import tpu as pltpu
from jax.sharding import PartitionSpec as P

LANES = 128
QUARTER = 32
BLOCK_ROWS = 66
CHUNK = 512
WINDOW = 1280
HOP = 3
VMEM_GRANT = 20 << 20
MESH = pl.DeviceIdType.MESH
F32 = jnp.float32


def block_histogram(weights, local):
    iota = lax.broadcasted_iota(jnp.int32, (2 * LANES, local.shape[1]), 0)
    onehot = jnp.where(iota == local, 1.0, 0.0).astype(jnp.bfloat16)
    return lax.dot_general(
        weights, onehot, (((1,), (1,)), ((), ())), preferred_element_type=F32
    )


def weigh(knob_throws, resp, nominal_row):
    log_weight = jnp.dot(knob_throws, resp, preferred_element_type=F32)
    return (nominal_row * jnp.exp(log_weight)).astype(jnp.bfloat16)


def central_rows(nominal_row):
    return jnp.broadcast_to(nominal_row, (16, nominal_row.shape[1])).astype(jnp.bfloat16)


def rows_of(ref, start, count):
    return jnp.concatenate([ref[pl.ds(start + g, 1), :] for g in range(count)], axis=1)


def quarter_blocks(sums):
    row = lax.broadcasted_iota(jnp.int32, (8, LANES), 0)
    tail = sums[4 * QUARTER : 4 * QUARTER + 8]
    central = jnp.where(row == 0, tail[:, :LANES], tail[:, LANES:])[:2]
    for quarter in range(4):
        mine = sums[quarter * QUARTER : (quarter + 1) * QUARTER]
        block = jnp.concatenate([mine[:, :LANES], mine[:, LANES:], central], axis=0)
        yield quarter % 2, quarter // 2, block


def windows_kernel(
    resp_hbm, bins_hbm, nominal_hbm, throws_hbm,
    resp_of, local_of, nominal_of, throws_t, extra,
    resp, bins, nominal, throws, nominal_rows, acc, starts, sems, resp_sems,
):
    nz = resp_of.shape[0]
    per_row = LANES
    rows = bins_hbm.shape[0]
    window = WINDOW // LANES
    loads = [
        pltpu.make_async_copy(src, dst, sems.at[i])
        for i, (src, dst) in enumerate(
            [(bins_hbm, bins), (nominal_hbm, nominal), (throws_hbm, throws)]
        )
    ]
    for load in loads:
        load.start()

    def clear(zb, carry):
        extra[:, zb] = jnp.zeros((2, 2, BLOCK_ROWS, LANES), F32)
        return carry

    lax.fori_loop(0, nz, clear, 0)
    for load in loads:
        load.wait()
    all_bins = bins[...]
    below = [jnp.int32(0)]
    for zb in range(1, nz):
        hits = jnp.sum(jnp.where(all_bins < zb * 2 * LANES, 1.0, 0.0), axis=0, keepdims=True)
        below.append(jnp.sum(hits).astype(jnp.int32))
    below.append(jnp.int32(rows * LANES))
    beyond = jnp.int32(0)
    for zb in range(nz):
        start = jnp.minimum(below[zb] // LANES, rows - window)
        starts[zb] = start
        beyond = jnp.maximum(beyond, below[zb + 1] - (start + window) * LANES)

    def resp_copy(zb):
        events = pl.ds(pl.multiple_of(starts[zb] * LANES, LANES), WINDOW)
        return pltpu.make_async_copy(resp_hbm.at[:, events], resp_of.at[zb], resp_sems.at[zb])

    def start_copy(zb, carry):
        resp_copy(zb).start()
        return carry

    lax.fori_loop(0, nz, start_copy, 0)
    nominal_rows[...] = nominal[...].astype(F32)
    knob_throws = throws[...].astype(F32).T.astype(jnp.bfloat16)
    throws_t[...] = knob_throws

    def take(zb, carry):
        at = starts[zb]
        for g in range(window):
            lanes = slice(g * LANES, (g + 1) * LANES)
            local_of[zb, :, lanes] = bins[pl.ds(at + g, 1), :] - zb * 2 * LANES
            nominal_of[zb, :, lanes] = nominal_rows[pl.ds(at + g, 1), :]
        return carry

    lax.fori_loop(0, nz, take, 0)

    @pl.when(beyond > 0)
    def _():
        copy = pltpu.make_async_copy(resp_hbm, resp, sems.at[3])
        copy.start()
        copy.wait()
        count = CHUNK // LANES

        def one_block(zb, carry):
            acc[...] = jnp.zeros(acc.shape, F32)
            first = starts[zb] + window

            def one_chunk(row, c):
                at = jnp.minimum(row, rows - count)
                nominal_row = rows_of(nominal_rows, at, count)
                events = pl.ds(pl.multiple_of(at * LANES, LANES), CHUNK)
                index = at * LANES + lax.broadcasted_iota(jnp.int32, (1, CHUNK), 1)
                bin_row = jnp.where(index >= row * LANES, rows_of(bins, at, count), -1)
                all_weights = jnp.concatenate(
                    [weigh(knob_throws, resp[:, events], nominal_row), central_rows(nominal_row)],
                    axis=0,
                )
                acc[...] += block_histogram(all_weights, bin_row - zb * 2 * LANES)
                return c

            def step(i, c):
                row = first + i * count

                @pl.when(row < rows)
                def _():
                    @pl.when(bins_row_min(bins, row) < (zb + 1) * 2 * LANES)
                    def _():
                        one_chunk(row, 0)

                return c

            lax.fori_loop(0, rows // count, step, 0)
            for c, x, block in quarter_blocks(acc[...]):
                extra[c, zb, x] = block
            return carry

        lax.fori_loop(0, nz, one_block, 0)

    def wait_copy(zb, carry):
        resp_copy(zb).wait()
        return carry

    lax.fori_loop(0, nz, wait_copy, 0)


def bins_row_min(bins, row):
    return jnp.min(bins[pl.ds(row, 1), :])


def windows(responses, bins, nominal, throws, nz):
    rows = bins.shape[0]
    hbm = pl.BlockSpec(memory_space=pltpu.HBM)
    vmem = pl.BlockSpec(memory_space=pltpu.VMEM)
    shape = jax.ShapeDtypeStruct
    return pl.pallas_call(
        windows_kernel,
        out_shape=(
            shape((nz, responses.shape[0], WINDOW), responses.dtype),
            shape((nz, 1, WINDOW), jnp.int32),
            shape((nz, 1, WINDOW), F32),
            shape(throws.shape[::-1], jnp.bfloat16),
            shape((2, nz, 2, BLOCK_ROWS, LANES), F32),
        ),
        in_specs=[hbm] * 4,
        out_specs=(vmem,) * 5,
        scratch_shapes=[
            pltpu.VMEM(responses.shape, responses.dtype),
            pltpu.VMEM(bins.shape, jnp.int32),
            pltpu.VMEM(nominal.shape, nominal.dtype),
            pltpu.VMEM(throws.shape, throws.dtype),
            pltpu.VMEM((rows, LANES), F32),
            pltpu.VMEM((4 * QUARTER + 16, 2 * LANES), F32),
            pltpu.SMEM((nz,), jnp.int32),
            pltpu.SemaphoreType.DMA((4,)),
            pltpu.SemaphoreType.DMA((nz,)),
        ],
        compiler_params=pltpu.CompilerParams(vmem_limit_bytes=VMEM_GRANT),
        name="windows",
    )(responses, bins, nominal, throws)


def exchange_kernel(
    nz, nu, spec_scale, cov_scale,
    resp_of, local_of, nominal_of, throws_t, extra,
    spectra, cov,
    part,
    core_in, summed, x_in, ring_out, ring_in, own, dev, blocks,
    rows_in, cols_in, spec_in, prod, prod_in, pack_out, pack_in,
    core_s, core_r, x_s, x_r, ring_s, ring_r,
    blk_s, blk_r, fwd_s, rows_r, cols_s, cols_r, spec_s, spec_r, tail_s, tail_r,
):
    ev = lax.axis_index("ev")
    u = lax.axis_index("uni")
    z = ev // 4
    xl = lax.rem(ev // 2, 2)
    c = lax.rem(ev, 2)
    core_ev = ev + 1 - 2 * c
    x_ev = ev + 2 - 4 * xl
    diag_ev = x_ev + 1 - 2 * c
    half = nz // 2
    slots = nz // nu
    relays = half // HOP

    def relay_of(d):
        return min((d + 1) // HOP, relays)

    targets = {r: [] for r in range(-relays, relays + 1)}
    for d in range(1 - half, half + 1):
        targets[relay_of(d)].append(d - HOP * relay_of(d))

    def along(d):
        return lax.rem(ev + 4 * (d % nz), 4 * nz)

    def z_at(d):
        return lax.rem(z + d % nz, nz)

    def send(src, dst, ssem, rsem, to_ev=ev, to_u=u):
        return pltpu.make_async_remote_copy(
            src_ref=src, dst_ref=dst, send_sem=ssem, recv_sem=rsem,
            device_id={"ev": to_ev, "uni": to_u}, device_id_type=MESH,
        )

    def still_to_go(d):
        end = max(d // HOP * HOP, 1)
        return 3.1 * (d - end) + 2.3 + 0.7 * end

    order = sorted(range(1, half + 1), key=lambda d: -still_to_go(d))
    away_of = [way * d for d in order for way in (1, -1) if way * d > -half] + [0]
    place = {d: k for k, d in enumerate(away_of)}

    def block_of(k):
        if isinstance(k, int):
            return z_at(away_of[k])
        away = sum(jnp.where(k == i, d % nz, 0) for i, d in enumerate(away_of))
        return lax.rem(z + away, nz)

    def tell(to_ev, to_u=u):
        pl.semaphore_signal(
            barrier, inc=1, device_id={"ev": to_ev, "uni": to_u}, device_id_type=MESH
        )

    barrier = pltpu.get_barrier_semaphore()
    peers = [core_ev, x_ev, diag_ev]
    for d in sorted({1} | {HOP * r for r in range(1, relays + 1)}):
        peers += [along(d), along(-d)]
    for peer in peers:
        tell(peer)
    for j in range(1, nu):
        tell(ev, lax.rem(u + j, nu))
    expected = len(peers) + nu - 1
    for slot in range(slots):
        d = lax.rem(z - (u * slots + slot) + nz + half - 1, nz) - (half - 1)
        relay = jnp.minimum((d + 1 + HOP * nz) // HOP - nz, relays)
        away = d - HOP * relay
        from_ev = lax.rem(ev + 4 * (nz - away), 4 * nz)

        def tell_column(v, carry, from_ev=from_ev):
            @pl.when((from_ev != ev) | (v != u))
            def _():
                tell(from_ev, v)

            return carry

        lax.fori_loop(0, nu, tell_column, 0)
    for r, aways in targets.items():
        for away in aways:
            if away == 0:
                expected = expected + jnp.where(z_at(-HOP * r) // slots == u, 0, 1)
            else:
                expected = expected + 1
    knob_throws = throws_t[...]
    pl.semaphore_wait(barrier, expected)

    def core_copy(k):
        zb = block_of(k)
        return send(part.at[1 - c, zb], core_in.at[zb], core_s.at[k], core_r.at[k], to_ev=core_ev)

    def x_copy(k):
        zb = block_of(k)
        return send(summed.at[zb, 1 - xl], x_in.at[zb], x_s.at[k], x_r.at[k], to_ev=x_ev)

    def histogram(k):
        zb = block_of(k)
        nominal_row = nominal_of[zb]
        weights = jnp.concatenate(
            [weigh(knob_throws, resp_of[zb], nominal_row), central_rows(nominal_row)], axis=0
        )
        sums = block_histogram(weights, local_of[zb])
        for to_core, to_x, block in quarter_blocks(sums):
            part[to_core, zb, to_x] = block + extra[to_core, zb, to_x]
        core_copy(k).start()

    def start_x(k):
        zb = block_of(k)
        core_copy(k).wait_recv()
        summed[zb] = part[c, zb] + core_in[zb]
        x_copy(k).start()

    def ring_copy(k):
        d = away_of[k]
        to = d if abs(d) == 1 or d % HOP == 0 else (1 if d > 0 else -1)
        return send(ring_out.at[k], ring_in.at[k], ring_s.at[k], ring_r.at[k], to_ev=along(to))

    def before(k):
        d = away_of[k]
        farther = d + (1 if d > 0 else -1)
        return place.get(farther) if farther % HOP else None

    def sum_step(k):
        zb = block_of(k)
        x_copy(k).wait_recv()
        value = summed[zb, xl] + x_in[zb]
        if before(k) is not None:
            ring_copy(before(k)).wait_recv()
            value = value + ring_in[before(k)]
        ring_out[k] = value
        ring_copy(k).start()

    def block_step(k, carry):
        histogram(k)

        @pl.when(k > 1)
        def _():
            start_x(k - 2)

        return carry

    when = {}
    for k in sorted(range(nz - 1), key=lambda k: -abs(away_of[k])):
        when[k] = max(4.2 + 0.75 * k, when.get(before(k), 0.0) + 3.1)
    done = 0
    for k in sorted(when, key=when.get):
        count = min(nz, max(int(when[k] / 0.65), k + 3, done))
        if count > done:
            lax.fori_loop(done, count, block_step, 0)
        if count == nz and done < nz:
            start_x(nz - 2)
            start_x(nz - 1)
        done = count
        sum_step(k)
    x_copy(nz - 1).wait_recv()
    total = summed[z, xl] + x_in[z]
    for k in range(nz - 1):
        if abs(away_of[k]) == 1 or away_of[k] % HOP == 0:
            ring_copy(k).wait_recv()
            total = total + ring_in[k]
    own[...] = total
    dev[:QUARTER] = total[:QUARTER] - total[2 * QUARTER : 2 * QUARTER + 1]
    dev[QUARTER:] = total[QUARTER : 2 * QUARTER] - total[2 * QUARTER + 1 : 2 * QUARTER + 2]

    def relay_copy(r, src):
        n = 2 * (abs(r) - 1) + (r < 0)
        return send(
            src, blocks.at[n], blk_s.at[n], blk_r.at[n], to_ev=along(HOP if r > 0 else -HOP)
        )

    def direct(r, src, waiting=False):
        origin = z_at(-HOP * r)
        owner = origin // slots
        slot = lax.rem(origin, slots)
        for away in sorted(targets[r], key=abs, reverse=True):
            n = HOP * r + away + half - 1
            copy = send(
                src, rows_in.at[slot, u], fwd_s.at[n], rows_r.at[slot, u],
                to_ev=along(away), to_u=owner,
            )
            run = copy.wait_send if waiting else copy.start
            if away:
                run()
                continue
            pl.when(owner != u)(run)
            if not waiting:

                @pl.when(owner == u)
                def _():
                    rows_in[slot, u] = src[...]

    if relays:
        relay_copy(1, dev).start()
        relay_copy(-1, dev).start()

    def cols_copy(j):
        return send(dev, cols_in.at[u], cols_s.at[j], cols_r.at[u], to_u=lax.rem(u + j, nu))

    def start_cols(j, carry):
        cols_copy(j).start()
        return carry

    direct(0, dev)
    lax.fori_loop(1, nu, start_cols, 0)
    cols_in[u] = dev[...]

    mine = 2 * xl + c
    spec_peers = ((core_ev, xl), (x_ev, 1 - xl), (diag_ev, 1 - xl))

    def spec_copy(i):
        peer, peer_half = spec_peers[i]
        src = own.at[pl.ds(pl.multiple_of(peer_half * QUARTER, QUARTER), QUARTER)]
        return send(src, spec_in.at[mine], spec_s.at[i], spec_r.at[i], to_ev=peer)

    for i in range(3):
        spec_copy(i).start()
    spec_in[mine] = own[pl.ds(pl.multiple_of(xl * QUARTER, QUARTER), QUARTER)]

    def block_of_relay(r):
        return blocks.at[2 * (abs(r) - 1) + (r < 0)]

    for r in range(1, relays + 1):
        for relay in (r, -r):
            relay_copy(relay, dev).wait_recv()
            if r < relays:
                relay_copy(relay + (1 if relay > 0 else -1), block_of_relay(relay)).start()
            else:
                direct(relay, block_of_relay(relay))
        if r < relays:
            for relay in (r, -r):
                direct(relay, block_of_relay(relay))

    for i in range(3):
        spec_copy(i).wait_recv()
    by_bin = spec_in[...].reshape(4 * QUARTER, LANES).T
    spectra[...] = jnp.where(c == 0, by_bin[: LANES // 2], by_bin[LANES // 2 :]) * spec_scale

    def wait_cols(j, carry):
        v = lax.rem(u + j, nu)
        send(dev, cols_in.at[v], cols_s.at[j], cols_r.at[v], to_u=v).wait_recv()
        return carry

    lax.fori_loop(1, nu, wait_cols, 0)

    depth = nu * QUARTER
    bf16 = jnp.bfloat16
    lane = lax.broadcasted_iota(jnp.int32, (depth, LANES), 1)
    left = cols_in[:, :QUARTER].reshape(depth, LANES)
    right = cols_in[:, QUARTER:].reshape(depth, LANES)
    cols = jnp.concatenate(
        [
            jnp.where(lane < LANES // 2, left, pltpu.roll(right, LANES // 2, 1)).T,
            jnp.where(lane < LANES // 2, pltpu.roll(left, LANES // 2, 1), right).T,
        ],
        axis=0,
    )
    cols_hi = cols.astype(bf16)
    cols_lo = (cols - cols_hi.astype(F32)).astype(bf16)
    cols_all = jnp.concatenate([cols_hi, cols_hi, cols_lo], axis=1)
    xl_rows = pl.ds(pl.multiple_of((1 - xl) * (LANES // 2), LANES // 2), LANES // 2)
    my_rows = pl.ds(pl.multiple_of(xl * (LANES // 2), LANES // 2), LANES // 2)

    def core_tail(slot, h):
        return send(
            prod.at[slot, h, 1 - c], prod_in.at[slot, h],
            tail_s.at[0, slot, h], tail_r.at[0, slot, h], to_ev=core_ev,
        )

    def x_tail(slot, h):
        return send(
            pack_out.at[slot, h], pack_in.at[slot, h],
            tail_s.at[1, slot, h], tail_r.at[1, slot, h], to_ev=x_ev,
        )

    def local_rows(slot):
        d = lax.rem(z - (u * slots + slot) + nz + half - 1, nz) - (half - 1)
        relay = jnp.minimum((d + 1 + HOP * nz) // HOP - nz, relays)
        return d == HOP * relay

    from_below = lax.rem(z - u * slots + nz, nz) <= half
    for i in range(slots):
        slot = jnp.where(from_below, slots - 1 - i, i)

        def wait_rows(j, carry, slot=slot):
            v = lax.rem(u + j, nu)
            send(dev, rows_in.at[slot, v], cols_s.at[0], rows_r.at[slot, v], to_ev=core_ev).wait_recv()
            return carry

        @pl.when(jnp.logical_not(local_rows(slot)))
        def _(wait_rows=wait_rows):
            wait_rows(0, 0)

        lax.fori_loop(1, nu, wait_rows, 0)
        for h in range(2):
            rows = rows_in[slot, :, h * QUARTER : (h + 1) * QUARTER].reshape(depth, LANES)
            rows_hi = rows.astype(bf16)
            rows_lo = (rows - rows_hi.astype(F32)).astype(bf16)
            rows_all = jnp.concatenate([rows_hi, rows_lo, rows_hi], axis=0)
            product = jnp.dot(cols_all, rows_all, preferred_element_type=F32)
            prod[slot, h, 0] = product[:LANES]
            prod[slot, h, 1] = product[LANES:]
            core_tail(slot, h).start()
    for i in range(slots):
        slot = jnp.where(from_below, slots - 1 - i, i)
        for h in range(2):
            core_tail(slot, h).wait_recv()
            pack_out[slot, h] = prod[slot, h, c, xl_rows] + prod_in[slot, h, xl_rows]
            x_tail(slot, h).start()
    for slot in range(slots):
        for h in range(2):
            x_tail(slot, h).wait_recv()
            keep = prod[slot, h, c, my_rows] + prod_in[slot, h, my_rows]
            at = (2 * slot + h) * LANES
            cov[:, at : at + LANES] = (keep + pack_in[slot, h]) * cov_scale

    def drain(k, carry):
        core_copy(k).wait_send()
        x_copy(k).wait_send()
        return carry

    lax.fori_loop(0, nz, drain, 0)

    for k in range(nz - 1):
        ring_copy(k).wait_send()
    for r in range(-relays, relays + 1):
        if r:
            relay_copy(r, dev).wait_send()
        direct(r, dev, waiting=True)

    def drain_cols(j, carry):
        cols_copy(j).wait_send()
        return carry

    lax.fori_loop(1, nu, drain_cols, 0)
    for i in range(3):
        spec_copy(i).wait_send()
    for slot in range(slots):
        for h in range(2):
            core_tail(slot, h).wait_send()
            x_tail(slot, h).wait_send()


def exchange(taken, nz, nu, spec_scale, cov_scale):
    slots = nz // nu
    rows = slots * 2 * LANES
    block = (BLOCK_ROWS, LANES)
    blk = (2 * QUARTER, LANES)
    vmem = pl.BlockSpec(memory_space=pltpu.VMEM)

    def buf(*shape):
        return pltpu.VMEM(shape, F32)

    def dma(*shape):
        return pltpu.SemaphoreType.DMA(shape)

    spectra, cov = pl.pallas_call(
        functools.partial(exchange_kernel, nz, nu, spec_scale, cov_scale),
        out_shape=(
            jax.ShapeDtypeStruct((LANES // 2, 4 * QUARTER), F32),
            jax.ShapeDtypeStruct((LANES // 2, rows), F32),
        ),
        in_specs=[vmem] * len(taken),
        out_specs=(vmem, vmem),
        scratch_shapes=[
            buf(2, nz, 2, *block),
            buf(nz, 2, *block),
            buf(nz, 2, *block),
            buf(nz, *block),
            buf(nz - 1, *block), buf(nz - 1, *block),
            buf(*block), buf(*blk),
            buf(2 * max(1, nz // 2 // HOP), *blk),
            buf(slots, nu, *blk), buf(nu, *blk),
            buf(4, QUARTER, LANES),
            buf(slots, 2, 2, LANES, LANES), buf(slots, 2, LANES, LANES),
            buf(slots, 2, LANES // 2, LANES), buf(slots, 2, LANES // 2, LANES),
            dma(nz), dma(nz), dma(nz), dma(nz),
            dma(nz - 1), dma(nz - 1),
            dma(2 * max(1, nz // 2 // HOP)), dma(2 * max(1, nz // 2 // HOP)),
            dma(nz), dma(slots, nu), dma(nu), dma(nu),
            dma(3), dma(3), dma(2, slots, 2), dma(2, slots, 2),
        ],
        compiler_params=pltpu.CompilerParams(
            collective_id=0, has_side_effects=True, vmem_limit_bytes=VMEM_GRANT
        ),
        name="exchange",
    )(*taken)
    return spectra, cov.T


def body(responses, event_bins, nominal_weight, throws):
    nz = lax.axis_size("ev") // 4
    nu = lax.axis_size("uni")
    bins_total = nz * 2 * LANES
    per_bin = event_bins.shape[0] * lax.axis_size("ev") // bins_total
    universes = throws.shape[1] * nu
    rows = event_bins.shape[0] // LANES
    inputs = [
        pltpu.with_memory_space_constraint(x, pltpu.HBM)
        for x in (
            responses, event_bins.reshape(rows, LANES), nominal_weight.reshape(rows, LANES), throws
        )
    ]
    taken = windows(*inputs, nz)
    return exchange(taken, nz, nu, 1.0 / per_bin, 1.0 / (universes * per_bin))


def solution(mesh):
    in_specs = (P(None, "ev"), P("ev"), P("ev"), P(None, "uni"))
    out_specs = (P("ev", "uni"), P("uni", "ev"))
    return jax.shard_map(body, mesh=mesh, in_specs=in_specs, out_specs=out_specs, check_vma=False)
```
